128 devices in a mesh: row: 8 (over x, y_hi), col: 16 (over z, y_lo, core).
Axes of the slice: x: 4, y: 4 (y_hi: 2, y_lo: 2; y = y_hi * 2 + y_lo), z: 4, core: 2. Of those that a mesh axis runs over, the one named last changes fastest.
Arguments:
- density: float32 [5120, 5120], P('row', 'col'), as said below
- pattern: int32 [80, 80], P('row', 'col'), may hold values from 0 to 1, as said below
- weights: float32 [5120], P('row'), may hold values from 0.5 to 5
Outputs:
- purified: float32 [5120, 5120], P('row', 'col')
- checks: float32 [2, 5120], P(None, 'col')
The draws below stay inside these ranges and needn't reach their ends.
Inputs may be any that keep to these rules, and one draw needn't show every extreme that they name: pattern is symmetric, and every block with |a - b| <= 2 is nonzero; the number of nonzero blocks differs strongly between block rows. density is symmetric and zero outside the blocks that pattern marks.
All inputs are finite; a program needn't handle non-finite values.
Results may differ from the reference program's by a relative error of at most 0.00012.
Values sent between devices are 32-bit elements; how exact they have to be, the bound alone decides.
A program may use at most 64 MiB of HBM per device.

```python
import math
import jax
import jax.numpy as jnp
from jax import lax

BLK = 64
ITERS = 1
NB = 80
N = 5120


def pattern_helper(key):
    base = jax.random.fold_in(key, 11)
    first_key, second_key = jax.random.split(base)
    limits = jax.random.randint(first_key, (NB,), 5, 45)
    rolled = jax.random.randint(second_key, (NB, NB), 0, 100)
    rolled = jnp.minimum(rolled, rolled.T)
    bound = jnp.minimum(limits[:, None], limits[None, :])
    index = jnp.arange(NB)
    banded = jnp.abs(index[:, None] - index[None, :]) <= 2
    return jnp.where(banded | (rolled < bound), 1, 0).astype(jnp.int32)


def draw_pattern(key, part):
    return pattern_helper(key)


def draw_density(key, part):
    blocks = pattern_helper(key)
    block_mask = jnp.repeat(jnp.repeat(blocks.astype(jnp.float32), BLK, axis=0), BLK, axis=1)
    noise_key = jax.random.fold_in(key, 23)
    raw = jax.random.normal(noise_key, (N, N), jnp.float32)
    sym = (raw + raw.T) * math.sqrt(0.5)
    sigma = 0.22 / math.sqrt(BLK * NB * 0.35)
    ident = jnp.eye(N, dtype=jnp.float32)
    return (block_mask * (0.5 * ident + sigma * sym)).astype(jnp.float32)


def block_scale(key, dims, pieces, smallest, high):
    gain, own = 1.0, jax.random.fold_in(key, 6)
    for position, shards_of in pieces:
        steps = jnp.exp(jax.random.uniform(jax.random.fold_in(own, position), (shards_of,), jnp.float32, smallest / len(pieces), high / len(pieces)))
        gain = gain * jnp.repeat(steps, dims[position] // shards_of).reshape([-1 if axis == position else 1 for axis in range(len(dims))])
    return gain


def setup_inputs(seed: int = 0) -> dict:
    key_of = jax.random.split(jax.random.key(seed), 4)
    density = draw_density(jax.random.fold_in(key_of[3], 71), 0)
    pattern = draw_pattern(jax.random.fold_in(key_of[3], 71), 0)
    weights = jnp.clip(jnp.exp(math.log(5.0) - 2.3025851 * jax.random.uniform(key_of[2], (N,), jnp.float32) ** block_scale(key_of[2], (N,), ((0, 8),), -0.2, 0.2)), 0.5, 5.0)
    return {"density": density, "pattern": pattern, "weights": weights}


def expand_mask(pattern):
    return jnp.repeat(jnp.repeat(pattern.astype(jnp.float32), BLK, axis=0), BLK, axis=1)


def full_dot(first, second):
    return jnp.dot(first, second, precision=lax.Precision.HIGHEST, preferred_element_type=jnp.float32)


def reference(density, pattern, weights):
    block_mask = expand_mask(pattern)
    current = density
    weight_row = weights[None, :]
    checks = []
    for iteration in range(ITERS):
        checks.append(full_dot(full_dot(weight_row, current), current))
        square = block_mask * full_dot(current, current)
        checks.append(full_dot(full_dot(weight_row, square), current))
        cube_term = block_mask * full_dot(square, current)
        current = 3.0 * square - 2.0 * cube_term
    return current, jnp.concatenate(checks, axis=0)
```

```python
import jax
import jax.numpy as jnp
from jax import lax
from jax.experimental import pallas as pl
from jax.experimental.pallas import tpu as pltpu
from jax.sharding import PartitionSpec as P

BLK = 64
MESH = pl.DeviceIdType.MESH
ROWS, COLS = 640, 320
NROW, NCOL = 8, 16
HALF = COLS // 2
YQ = 64
SEMS = 112


def split(value):
    high = value.astype(jnp.bfloat16)
    low = (value - high.astype(jnp.float32)).astype(jnp.bfloat16)
    return high, low


def kernel(dens, pat, wts, out, chk, dcol, drow, srow, hop, acc, chk_out, chk_in, send, recv):
    row, col = lax.axis_index("row"), lax.axis_index("col")
    x, yh = row // 2, row % 2
    z, yl, core = col // 4, (col // 2) % 2, col % 2

    def dev(x_, yh_, z_, yl_, core_):
        return (x_ * 2 + yh_, (z_ * 2 + yl_) * 2 + core_)

    def step(value, by):
        return (value + by) % 4

    xp, xm = dev(step(x, 1), yh, z, yl, core), dev(step(x, 3), yh, z, yl, core)
    zp, zm = dev(x, yh, step(z, 1), yl, core), dev(x, yh, step(z, 3), yl, core)
    ya = dev(x, yh, z, 1 - yl, core)
    yb = dev(x, 1 - yh, z, 1 - yl, core)
    mate = dev(x, yh, z, yl, 1 - core)
    rows_of = [((row + i) % NROW, col) for i in range(1, NROW)]

    barrier = pltpu.get_barrier_semaphore()
    for peer in rows_of + [zp, zm, ya, yb, mate]:
        pl.semaphore_signal(barrier, inc=1, device_id=peer, device_id_type=MESH)

    tile = dens[...].T
    dcol[row] = tile
    drow[col] = tile
    rm = (lax.broadcasted_iota(jnp.int32, (NROW * 2, ROWS), 0)
          == lax.broadcasted_iota(jnp.int32, (NROW * 2, ROWS), 1) // BLK)
    cm = (lax.broadcasted_iota(jnp.int32, (COLS, 8), 1)
          == lax.broadcasted_iota(jnp.int32, (COLS, 8), 0) // BLK)
    nr, nc = ROWS // BLK, COLS // BLK
    pat_t = pat[...].astype(jnp.float32)
    part = lax.dot_general(cm[:, :nc].astype(jnp.float32), pat_t, (((1,), (1,)), ((), ())),
                           preferred_element_type=jnp.float32)
    mask = jnp.dot(part, rm[:nr].astype(jnp.float32), preferred_element_type=jnp.float32)

    pl.semaphore_wait(barrier, len(rows_of) + 5)

    copies = {}

    def put(name, src, dst, device):
        i = len(copies)
        copies[name] = pltpu.make_async_remote_copy(
            src_ref=src, dst_ref=dst, send_sem=send.at[i], recv_sem=recv.at[i],
            device_id=device, device_id_type=MESH)
        copies[name].start()

    def got(*names):
        for name in names:
            copies[name].wait_recv()

    def slot(z_, yl_, core_):
        return (z_ * 2 + yl_) * 2 + core_

    mine, mine_p = slot(z, yl, core), slot(z, 1 - yl, core)
    back, ahead, far = slot(step(z, 3), yl, core), slot(step(z, 1), yl, core), slot(step(z, 2), yl, core)
    back_p, ahead_p, far_p = (slot(step(z, 3), 1 - yl, core), slot(step(z, 1), 1 - yl, core),
                              slot(step(z, 2), 1 - yl, core))

    def half(buf, s, h):
        return buf.at[s, pl.ds(h * HALF, HALF), :]

    def same(name, ref, device):
        put(name, ref, ref, device)

    same("z+0", half(drow, mine, 0), zp)
    same("z-1", half(drow, mine, 1), zm)
    same("x+0", half(dcol, row, 0), xp)
    same("x-1", half(dcol, row, 1), xm)
    put("ya0", half(dcol, row, 0), hop.at[0], ya)
    put("yb1", half(dcol, row, 1), hop.at[1], yb)
    same("z+1", half(drow, mine, 1), zp)
    same("z-0", half(drow, mine, 0), zm)
    same("x+1", half(dcol, row, 1), xp)
    same("x-0", half(dcol, row, 0), xm)
    same("y0", half(drow, mine, 0), ya)
    same("c0", drow.at[mine], mate)

    def rowslot(x_, yh_):
        return x_ * 2 + yh_

    got("z+0")
    same("zz+", half(drow, back, 0), zp)
    got("z-1")
    same("zz-", half(drow, ahead, 1), zm)
    got("x+0")
    same("xx+", half(dcol, rowslot(step(x, 3), yh), 0), xp)
    got("x-1")
    same("xx-", half(dcol, rowslot(step(x, 1), yh), 1), xm)
    got("ya0")
    put("yab", hop.at[0], half(dcol, rowslot(x, yh), 0), yb)
    got("yb1")
    put("yba", hop.at[1], half(dcol, rowslot(x, 1 - yh), 1), ya)
    same("y1", half(drow, mine, 1), ya)
    rp = rowslot(x, 1 - yh)
    got("yab")
    same("xp+0", half(dcol, rp, 0), xp)
    same("xp-0", half(dcol, rp, 0), xm)
    got("y0")
    same("zp+0", half(drow, mine_p, 0), zp)
    same("zp-0", half(drow, mine_p, 0), zm)
    got("z+1")
    same("c1", drow.at[back], mate)
    got("z-0")
    same("c2", drow.at[ahead], mate)
    got("yba")
    same("xp+1", half(dcol, rp, 1), xp)
    same("xp-1", half(dcol, rp, 1), xm)
    got("zz+", "zz-")
    same("c3", drow.at[far], mate)
    got("y1")
    same("zp+1", half(drow, mine_p, 1), zp)
    same("zp-1", half(drow, mine_p, 1), zm)
    same("c4", drow.at[mine_p], mate)
    got("zp+0")
    same("zzp+", half(drow, back_p, 0), zp)
    got("xp+0")
    same("xxp+", half(dcol, rowslot(step(x, 3), 1 - yh), 0), xp)
    got("x+1", "x-0", "xx+", "xx-")
    got("zp-0", "zp-1")
    same("zzp-", half(drow, ahead_p, 1), zm)
    same("c6", drow.at[ahead_p], mate)
    got("xp-0", "xp-1")
    same("xxp-", half(dcol, rowslot(step(x, 1), 1 - yh), 1), xm)
    got("zp+1")
    same("c5", drow.at[back_p], mate)
    got("xp+1")
    got("c0", "c1", "c2", "c3", "c4", "c5", "c6")

    def product(panel, k):
        a_hi, a_lo = split(dcol[k])
        b_hi, b_lo = split(panel[pl.ds(2 * k, 2)].reshape(2 * COLS, ROWS))
        dot = lambda a, b: jnp.dot(a, b, preferred_element_type=jnp.float32)
        acc[...] += dot(a_hi, b_hi) + dot(a_hi, b_lo) + dot(a_lo, b_hi)

    def pick(i, values):
        k = values[-1]
        for j in reversed(range(len(values) - 1)):
            k = jnp.where(i == j, values[j], k)
        return k

    def products(panel, ks):
        if len(ks) == 1:
            product(panel, ks[0])
            return

        def run(i, carry):
            product(panel, pick(i, ks))
            return carry

        lax.fori_loop(0, len(ks), run, 0)

    d = (z - x + 4) % 4
    o0 = jnp.where(d == 2, step(x, 1), x)
    o1 = jnp.where(d <= 1, step(x, 1), step(x, 3))
    o2 = jnp.where(d == 0, step(x, 3), step(z, 2))
    o3 = step(x, 2)
    near, other = rowslot(o3, yh), rowslot(o2, 1 - yl)
    acc[...] = jnp.zeros_like(acc)
    products(drow, [rowslot(o0, yl), rowslot(o1, yl), rowslot(o0, 1 - yl), rowslot(o1, 1 - yl),
                    rowslot(o2, yl), jnp.where(d == 0, other, near)])
    got("zzp+", "zzp-")
    same("c7", drow.at[far_p], mate)
    got("xxp+", "xxp-")
    got("c7")
    products(drow, [jnp.where(d == 0, near, other), rowslot(o3, 1 - yh)])

    w8 = jnp.broadcast_to(wts[...], (8, ROWS))

    def column_sums(value):
        return lax.dot_general(w8, value, (((1,), (1,)), ((), ())),
                               precision=lax.Precision.HIGHEST, preferred_element_type=jnp.float32)

    square = acc[...]
    srow[col] = mask * square
    chk_out[0] = column_sums(square)

    def own(s, h):
        return srow.at[s, pl.ds(h * HALF, HALF), :]

    def late(s, h):
        return srow.at[s, pl.ds(h * HALF, YQ), :]

    def early(s, h):
        return srow.at[s, pl.ds(h * HALF + YQ, HALF - YQ), :]

    same("sz+0", own(mine, 0), zp)
    same("sz-1", own(mine, 1), zm)
    same("sy0", early(mine, 0), ya)
    same("sz+1", own(mine, 1), zp)
    same("sz-0", own(mine, 0), zm)
    same("sy1", early(mine, 1), ya)
    same("sc0", srow.at[mine], mate)
    same("sq0", late(mine, 0), ya)
    same("sq1", late(mine, 1), ya)
    for i in range(1, NROW):
        put(f"k{i}", chk_out.at[0], chk_in.at[0, row], rows_of[i - 1])
    acc[...] = jnp.zeros_like(acc)
    got("sc0")
    products(srow, [rowslot(z, yl)])
    got("sz+0")
    same("szz+", own(back, 0), zp)
    got("sz-1")
    same("szz-", own(ahead, 1), zm)
    got("sy0")
    same("szp+0", early(mine_p, 0), zp)
    same("szp-0", early(mine_p, 0), zm)
    got("sy1")
    same("szp-1", early(mine_p, 1), zm)
    same("szp+1", early(mine_p, 1), zp)
    got("sz+1")
    same("sq2", late(back, 0), ya)
    same("sq3", late(back, 1), ya)
    same("sc1", srow.at[back], mate)
    got("sz-0")
    same("sq4", late(ahead, 0), ya)
    same("sq5", late(ahead, 1), ya)
    same("sc2", srow.at[ahead], mate)
    got("sq0", "sq1")
    same("sc4", srow.at[mine_p], mate)
    got("sc1", "sc2")
    products(srow, [rowslot(step(z, 3), yl), rowslot(step(z, 1), yl)])
    got("szz+", "szz-")
    same("sq6", late(far, 0), ya)
    same("sq7", late(far, 1), ya)
    same("sc3", srow.at[far], mate)
    got("szp+0")
    same("szzp+", early(back_p, 0), zp)
    got("szp-0", "szp-1")
    same("szzp-", early(ahead_p, 1), zm)
    got("sq4", "sq5")
    same("sc6", srow.at[ahead_p], mate)
    got("szp+1", "sq2", "sq3")
    same("sc5", srow.at[back_p], mate)
    got("sc3", "sc4", "sc5", "sc6")
    products(srow, [rowslot(step(z, 2), yl), rowslot(z, 1 - yl), rowslot(step(z, 1), 1 - yl),
                    rowslot(step(z, 3), 1 - yl)])
    got("szzp+", "szzp-", "sq6", "sq7")
    same("sc7", srow.at[far_p], mate)
    got("sc7")
    products(srow, [rowslot(step(z, 2), 1 - yl)])

    cube = acc[...]
    chk_out[1] = column_sums(cube)
    for i in range(1, NROW):
        put(f"l{i}", chk_out.at[1], chk_in.at[1, row], rows_of[i - 1])
    chk_in[0, row] = chk_out[0]
    chk_in[1, row] = chk_out[1]
    out[...] = (3.0 * srow[col] - 2.0 * (mask * cube)).T
    for i in range(1, NROW):
        got(f"k{i}", f"l{i}")
    total0, total1 = chk_in[0, 0], chk_in[1, 0]
    for i in range(1, NROW):
        total0 += chk_in[0, i]
        total1 += chk_in[1, i]
    chk[...] = jnp.concatenate([total0[:1], total1[:1]], axis=0)
    for copy in copies.values():
        copy.wait_send()
    assert len(copies) <= SEMS


def body(density, pattern, weights):
    f32 = jnp.float32
    vmem = pl.BlockSpec(memory_space=pltpu.VMEM)
    return pl.pallas_call(
        kernel,
        out_shape=(jax.ShapeDtypeStruct((ROWS, COLS), f32), jax.ShapeDtypeStruct((2, COLS), f32)),
        in_specs=[vmem] * 3,
        out_specs=(vmem, vmem),
        scratch_shapes=[
            pltpu.VMEM((NROW, COLS, ROWS), f32),
            pltpu.VMEM((NCOL, COLS, ROWS), f32),
            pltpu.VMEM((NCOL, COLS, ROWS), f32),
            pltpu.VMEM((2, HALF, ROWS), f32),
            pltpu.VMEM((COLS, ROWS), f32),
            pltpu.VMEM((2, 8, COLS), f32),
            pltpu.VMEM((2, NROW, 8, COLS), f32),
            pltpu.SemaphoreType.DMA((SEMS,)),
            pltpu.SemaphoreType.DMA((SEMS,)),
        ],
        compiler_params=pltpu.CompilerParams(
            collective_id=0, has_side_effects=True, vmem_limit_bytes=63 * 1024 * 1024),
        name="purify",
    )(density, pattern, weights[None, :])


def solution(mesh):
    in_specs = (P("row", "col"), P("row", "col"), P("row"))
    out_specs = (P("row", "col"), P(None, "col"))
    return jax.shard_map(body, mesh=mesh, in_specs=in_specs, out_specs=out_specs, check_vma=False)
```

```python
import jax
import jax.numpy as jnp
from jax import lax
from jax.experimental import pallas as pl
from jax.experimental.pallas import tpu as pltpu
from jax.sharding import PartitionSpec as P

BLK = 64
MESH = pl.DeviceIdType.MESH
ROWS, COLS = 640, 320
NROW, NCOL = 8, 16
HALF = COLS // 2
YQ = 64
SEMS = 112


def split(value):
    high = value.astype(jnp.bfloat16)
    low = (value - high.astype(jnp.float32)).astype(jnp.bfloat16)
    return high, low


def kernel(dens, pat, wts, out, chk, dcol, drow, srow, hop, acc, chk_out, chk_in, send, recv):
    row, col = lax.axis_index("row"), lax.axis_index("col")
    x, yh = row // 2, row % 2
    z, yl, core = col // 4, (col // 2) % 2, col % 2

    def dev(x_, yh_, z_, yl_, core_):
        return (x_ * 2 + yh_, (z_ * 2 + yl_) * 2 + core_)

    def step(value, by):
        return (value + by) % 4

    xp, xm = dev(step(x, 1), yh, z, yl, core), dev(step(x, 3), yh, z, yl, core)
    zp, zm = dev(x, yh, step(z, 1), yl, core), dev(x, yh, step(z, 3), yl, core)
    ya = dev(x, yh, z, 1 - yl, core)
    yb = dev(x, 1 - yh, z, 1 - yl, core)
    mate = dev(x, yh, z, yl, 1 - core)
    rows_of = [((row + i) % NROW, col) for i in range(1, NROW)]

    barrier = pltpu.get_barrier_semaphore()
    for peer in rows_of + [zp, zm, ya, yb, mate]:
        pl.semaphore_signal(barrier, inc=1, device_id=peer, device_id_type=MESH)

    tile = dens[...]
    dcol[row] = tile
    drow[col] = tile
    rm = (lax.broadcasted_iota(jnp.int32, (NROW * 2, ROWS), 0)
          == lax.broadcasted_iota(jnp.int32, (NROW * 2, ROWS), 1) // BLK)
    cm = (lax.broadcasted_iota(jnp.int32, (COLS, 8), 1)
          == lax.broadcasted_iota(jnp.int32, (COLS, 8), 0) // BLK)
    nr, nc = ROWS // BLK, COLS // BLK
    part = jnp.dot(cm[:, :nc].astype(jnp.float32), pat[...].astype(jnp.float32),
                   preferred_element_type=jnp.float32)
    mask = jnp.dot(part, rm[:nr].astype(jnp.float32), preferred_element_type=jnp.float32)

    pl.semaphore_wait(barrier, len(rows_of) + 5)

    copies = {}

    def put(name, src, dst, device):
        i = len(copies)
        copies[name] = pltpu.make_async_remote_copy(
            src_ref=src, dst_ref=dst, send_sem=send.at[i], recv_sem=recv.at[i],
            device_id=device, device_id_type=MESH)
        copies[name].start()

    def got(*names):
        for name in names:
            copies[name].wait_recv()

    def slot(z_, yl_, core_):
        return (z_ * 2 + yl_) * 2 + core_

    mine, mine_p = slot(z, yl, core), slot(z, 1 - yl, core)
    back, ahead, far = slot(step(z, 3), yl, core), slot(step(z, 1), yl, core), slot(step(z, 2), yl, core)
    back_p, ahead_p, far_p = (slot(step(z, 3), 1 - yl, core), slot(step(z, 1), 1 - yl, core),
                              slot(step(z, 2), 1 - yl, core))

    def half(buf, s, h):
        return buf.at[s, pl.ds(h * HALF, HALF), :]

    def same(name, ref, device):
        put(name, ref, ref, device)

    same("z+0", half(drow, mine, 0), zp)
    same("z-1", half(drow, mine, 1), zm)
    same("x+0", half(dcol, row, 0), xp)
    same("x-1", half(dcol, row, 1), xm)
    put("ya0", half(dcol, row, 0), hop.at[0], ya)
    put("yb1", half(dcol, row, 1), hop.at[1], yb)
    same("z+1", half(drow, mine, 1), zp)
    same("z-0", half(drow, mine, 0), zm)
    same("x+1", half(dcol, row, 1), xp)
    same("x-0", half(dcol, row, 0), xm)
    same("y0", half(drow, mine, 0), ya)
    same("c0", drow.at[mine], mate)

    def rowslot(x_, yh_):
        return x_ * 2 + yh_

    got("z+0")
    same("zz+", half(drow, back, 0), zp)
    got("z-1")
    same("zz-", half(drow, ahead, 1), zm)
    got("x+0")
    same("xx+", half(dcol, rowslot(step(x, 3), yh), 0), xp)
    got("x-1")
    same("xx-", half(dcol, rowslot(step(x, 1), yh), 1), xm)
    got("ya0")
    put("yab", hop.at[0], half(dcol, rowslot(x, yh), 0), yb)
    got("yb1")
    put("yba", hop.at[1], half(dcol, rowslot(x, 1 - yh), 1), ya)
    same("y1", half(drow, mine, 1), ya)
    rp = rowslot(x, 1 - yh)
    got("yab")
    same("xp+0", half(dcol, rp, 0), xp)
    same("xp-0", half(dcol, rp, 0), xm)
    got("y0")
    same("zp+0", half(drow, mine_p, 0), zp)
    same("zp-0", half(drow, mine_p, 0), zm)
    got("z+1")
    same("c1", drow.at[back], mate)
    got("z-0")
    same("c2", drow.at[ahead], mate)
    got("yba")
    same("xp+1", half(dcol, rp, 1), xp)
    same("xp-1", half(dcol, rp, 1), xm)
    got("zz+", "zz-")
    same("c3", drow.at[far], mate)
    got("y1")
    same("zp+1", half(drow, mine_p, 1), zp)
    same("zp-1", half(drow, mine_p, 1), zm)
    same("c4", drow.at[mine_p], mate)
    got("zp+0")
    same("zzp+", half(drow, back_p, 0), zp)
    got("xp+0")
    same("xxp+", half(dcol, rowslot(step(x, 3), 1 - yh), 0), xp)
    got("x+1", "x-0", "xx+", "xx-")
    got("zp-0", "zp-1")
    same("zzp-", half(drow, ahead_p, 1), zm)
    same("c6", drow.at[ahead_p], mate)
    got("xp-0", "xp-1")
    same("xxp-", half(dcol, rowslot(step(x, 1), 1 - yh), 1), xm)
    got("zp+1")
    same("c5", drow.at[back_p], mate)
    got("xp+1")
    got("c0", "c1", "c2", "c3", "c4", "c5", "c6")

    def product(panel, k):
        a_hi, a_lo = split(dcol[k])
        b_hi, b_lo = split(panel[pl.ds(2 * k, 2)].reshape(2 * COLS, ROWS))
        dot = lambda a, b: jnp.dot(a, b, preferred_element_type=jnp.float32)
        acc[...] += dot(a_hi, b_hi) + dot(a_hi, b_lo) + dot(a_lo, b_hi)

    def pick(i, values):
        k = values[-1]
        for j in reversed(range(len(values) - 1)):
            k = jnp.where(i == j, values[j], k)
        return k

    def products(panel, ks):
        if len(ks) == 1:
            product(panel, ks[0])
            return

        def run(i, carry):
            product(panel, pick(i, ks))
            return carry

        lax.fori_loop(0, len(ks), run, 0)

    d = (z - x + 4) % 4
    o0 = jnp.where(d == 2, step(x, 1), x)
    o1 = jnp.where(d <= 1, step(x, 1), step(x, 3))
    o2 = jnp.where(d == 0, step(x, 3), step(z, 2))
    o3 = step(x, 2)
    near, other = rowslot(o3, yh), rowslot(o2, 1 - yl)
    acc[...] = jnp.zeros_like(acc)
    products(drow, [rowslot(o0, yl), rowslot(o1, yl), rowslot(o0, 1 - yl), rowslot(o1, 1 - yl),
                    rowslot(o2, yl), jnp.where(d == 0, other, near)])
    got("zzp+", "zzp-")
    same("c7", drow.at[far_p], mate)
    got("xxp+", "xxp-")
    got("c7")
    products(drow, [jnp.where(d == 0, near, other), rowslot(o3, 1 - yh)])

    w8 = jnp.broadcast_to(wts[...][None, :], (8, ROWS))

    def column_sums(value):
        return lax.dot_general(w8, value, (((1,), (1,)), ((), ())),
                               precision=lax.Precision.HIGHEST, preferred_element_type=jnp.float32)

    square = acc[...]
    srow[col] = mask * square
    chk_out[0] = column_sums(square)

    def own(s, h):
        return srow.at[s, pl.ds(h * HALF, HALF), :]

    def late(s, h):
        return srow.at[s, pl.ds(h * HALF, YQ), :]

    def early(s, h):
        return srow.at[s, pl.ds(h * HALF + YQ, HALF - YQ), :]

    same("sz+0", own(mine, 0), zp)
    same("sz-1", own(mine, 1), zm)
    same("sy0", early(mine, 0), ya)
    same("sz+1", own(mine, 1), zp)
    same("sz-0", own(mine, 0), zm)
    same("sy1", early(mine, 1), ya)
    same("sc0", srow.at[mine], mate)
    same("sq0", late(mine, 0), ya)
    same("sq1", late(mine, 1), ya)
    for i in range(1, NROW):
        put(f"k{i}", chk_out.at[0], chk_in.at[0, row], rows_of[i - 1])
    acc[...] = jnp.zeros_like(acc)
    got("sc0")
    products(srow, [rowslot(z, yl)])
    got("sz+0")
    same("szz+", own(back, 0), zp)
    got("sz-1")
    same("szz-", own(ahead, 1), zm)
    got("sy0")
    same("szp+0", early(mine_p, 0), zp)
    same("szp-0", early(mine_p, 0), zm)
    got("sy1")
    same("szp-1", early(mine_p, 1), zm)
    same("szp+1", early(mine_p, 1), zp)
    got("sz+1")
    same("sq2", late(back, 0), ya)
    same("sq3", late(back, 1), ya)
    same("sc1", srow.at[back], mate)
    got("sz-0")
    same("sq4", late(ahead, 0), ya)
    same("sq5", late(ahead, 1), ya)
    same("sc2", srow.at[ahead], mate)
    got("sq0", "sq1")
    same("sc4", srow.at[mine_p], mate)
    got("sc1", "sc2")
    products(srow, [rowslot(step(z, 3), yl), rowslot(step(z, 1), yl)])
    got("szz+", "szz-")
    same("sq6", late(far, 0), ya)
    same("sq7", late(far, 1), ya)
    same("sc3", srow.at[far], mate)
    got("szp+0")
    same("szzp+", early(back_p, 0), zp)
    got("szp-0", "szp-1")
    same("szzp-", early(ahead_p, 1), zm)
    got("sq4", "sq5")
    same("sc6", srow.at[ahead_p], mate)
    got("szp+1", "sq2", "sq3")
    same("sc5", srow.at[back_p], mate)
    got("sc3", "sc4", "sc5", "sc6")
    products(srow, [rowslot(step(z, 2), yl), rowslot(z, 1 - yl), rowslot(step(z, 1), 1 - yl),
                    rowslot(step(z, 3), 1 - yl)])
    got("szzp+", "szzp-", "sq6", "sq7")
    same("sc7", srow.at[far_p], mate)
    got("sc7")
    products(srow, [rowslot(step(z, 2), 1 - yl)])

    cube = acc[...]
    chk_out[1] = column_sums(cube)
    for i in range(1, NROW):
        put(f"l{i}", chk_out.at[1], chk_in.at[1, row], rows_of[i - 1])
    chk_in[0, row] = chk_out[0]
    chk_in[1, row] = chk_out[1]
    out[...] = 3.0 * srow[col] - 2.0 * (mask * cube)
    for i in range(1, NROW):
        got(f"k{i}", f"l{i}")
    total0, total1 = chk_in[0, 0], chk_in[1, 0]
    for i in range(1, NROW):
        total0 += chk_in[0, i]
        total1 += chk_in[1, i]
    chk[...] = jnp.concatenate([total0[:1], total1[:1]], axis=0)
    for copy in copies.values():
        copy.wait_send()
    assert len(copies) <= SEMS


def body(density, pattern, weights):
    f32 = jnp.float32
    vmem = pl.BlockSpec(memory_space=pltpu.VMEM)
    purified, checks = pl.pallas_call(
        kernel,
        out_shape=(jax.ShapeDtypeStruct((COLS, ROWS), f32), jax.ShapeDtypeStruct((2, COLS), f32)),
        in_specs=[vmem] * 3,
        out_specs=(vmem, vmem),
        scratch_shapes=[
            pltpu.VMEM((NROW, COLS, ROWS), f32),
            pltpu.VMEM((NCOL, COLS, ROWS), f32),
            pltpu.VMEM((NCOL, COLS, ROWS), f32),
            pltpu.VMEM((2, HALF, ROWS), f32),
            pltpu.VMEM((COLS, ROWS), f32),
            pltpu.VMEM((2, 8, COLS), f32),
            pltpu.VMEM((2, NROW, 8, COLS), f32),
            pltpu.SemaphoreType.DMA((SEMS,)),
            pltpu.SemaphoreType.DMA((SEMS,)),
        ],
        compiler_params=pltpu.CompilerParams(
            collective_id=0, has_side_effects=True, vmem_limit_bytes=63 * 1024 * 1024),
        name="purify",
    )(density.T, pattern.T, weights)
    return purified.T, checks


def solution(mesh):
    in_specs = (P("row", "col"), P("row", "col"), P("row"))
    out_specs = (P("row", "col"), P(None, "col"))
    return jax.shard_map(body, mesh=mesh, in_specs=in_specs, out_specs=out_specs, check_vma=False)
```

```python
import jax
import jax.numpy as jnp
from jax import lax
from jax.experimental import pallas as pl
from jax.experimental.pallas import tpu as pltpu
from jax.sharding import PartitionSpec as P

BLK = 64
MESH = pl.DeviceIdType.MESH
ROWS, COLS = 640, 320
NROW, NCOL = 8, 16
SEMS = 240

LINK_ROW, LINK_LATENCY = 0.0545, 1.7
MATE_ROW, MATE_LATENCY = 0.0057, 1.0
LEAD = 3.0

PIECES_D = ((0, 80, "first", 1), (80, 80, "first", 1), (160, 80, "first", -1), (240, 80, "first", -1))
PIECES_S = ((0, 88, "first", 1), (88, 72, "after", 1), (160, 88, "first", -1), (248, 72, "after", -1))
GROUPS = ((0, 160), (160, 160))


class Plan:
    def __init__(self):
        self.items, self.made = {}, {}

    def add(self, name, link, rows, deps, do):
        if link == "work":
            length, latency = rows, 0.0
        elif link == "mate":
            length, latency = rows * MATE_ROW, MATE_LATENCY
        else:
            length, latency = rows * LINK_ROW, LINK_LATENCY
        self.items[name] = (link, length, latency, tuple(deps), do)

    def order(self):
        items = self.items
        after = {name: [] for name in items}
        for name, item in items.items():
            for dep in item[3]:
                after[dep].append(name)
        level = {}
        for name in reversed(list(items)):
            _, length, latency, _, _ = items[name]
            level[name] = length + latency + max([level[n] for n in after[name]], default=0.0)
        free, there, events = {}, {}, []
        left = list(items)
        while left:
            best = None
            for name in left:
                link, _, _, deps, _ = items[name]
                if all(dep in there for dep in deps):
                    ready = max([there[dep] for dep in deps], default=0.0)
                    key = (max(ready, free.get(link, 0.0)), -level[name], len(events))
                    if best is None or key < best[0]:
                        best = (key, name, ready)
            (start, _, _), name, ready = best
            link, length, latency, _, _ = items[name]
            free[link] = start + length
            there[name] = start + length + latency
            issue = start if link == "work" else max(ready, start - LEAD)
            events.append((issue, len(events), name))
            left.remove(name)
        return [name for _, _, name in sorted(events)], there

    def run(self, wait):
        done = set()
        for name in self.order()[0]:
            _, _, _, deps, do = self.items[name]
            for dep in deps:
                if dep not in done and self.items[dep][0] != "work":
                    wait(dep)
                    done.add(dep)
            do(name)
        for name in self.items:
            if name not in done and self.items[name][0] != "work":
                wait(name)


def ring(plan, tag, pieces, plus, minus, cross, send_to):
    fills = {slot: {} for slot in ("back", "ahead", "far", "mine_p", "back_p", "ahead_p", "far_p")}

    def over(name, src, dst, p, deps):
        first, rows = pieces[p][:2]
        last = deps
        for i, link in enumerate(cross(p)):
            step = f"{name}/{i}"
            plan.add(step, link, rows, last, send_to(step, link, src, dst, first, rows, i, p))
            last = [step]
        fills[dst][p] = last[0]
        return last

    def around(kind, p, deps, slots):
        mine, back, ahead, far = slots
        first, rows, _, way = pieces[p]
        names = {}
        for link, dst in ((plus, back), (minus, ahead)):
            name = f"{tag}{kind}{link}{p}"
            plan.add(name, link, rows, deps, send_to(name, link, mine, dst, first, rows, 0, p))
            fills[dst][p] = name
            names[link] = name
        link, src = (plus, back) if way > 0 else (minus, ahead)
        name = f"{tag}{kind}far{p}"
        plan.add(name, link, rows, [names[link]], send_to(name, link, src, far, first, rows, 0, p))
        fills[far][p] = name

    for p, (first, rows, when, way) in enumerate(pieces):
        around("own", p, [], ("mine", "back", "ahead", "far"))
        if when == "first":
            last = over(f"{tag}y{p}", "mine", "mine_p", p, [])
            around("par", p, last, ("mine_p", "back_p", "ahead_p", "far_p"))
        else:
            over(f"{tag}y{p}", "mine", "mine_p", p, [])
            for slot in ("back", "ahead", "far"):
                over(f"{tag}y{slot}{p}", slot, slot + "_p", p, [fills[slot][p]])
    return fills


def split(value):
    high = value.astype(jnp.bfloat16)
    low = (value - high.astype(jnp.float32)).astype(jnp.bfloat16)
    return high, low


def dot3(a, b):
    (a_hi, a_lo), (b_hi, b_lo) = split(a), split(b)
    dot = lambda u, v: jnp.dot(u, v, preferred_element_type=jnp.float32)
    return dot(a_hi, b_hi) + dot(a_hi, b_lo) + dot(a_lo, b_hi)


def kernel(dens, pat, wts, out, chk, dcol, drow, srow, hop, acc,
           sums_out, sums_in, parts_out, parts_in, send, recv):
    row, col = lax.axis_index("row"), lax.axis_index("col")
    x, yh = row // 2, row % 2
    z, yl, core = col // 4, (col // 2) % 2, col % 2

    def dev(x_, yh_, z_, yl_, core_):
        return (x_ * 2 + yh_, (z_ * 2 + yl_) * 2 + core_)

    def step(value, by):
        return (value + by) % 4

    def rowslot(x_, yh_):
        return x_ * 2 + yh_

    def colslot(z_, yl_):
        return (z_ * 2 + yl_) * 2 + core

    peer = {
        "x+": dev(step(x, 1), yh, z, yl, core), "x-": dev(step(x, 3), yh, z, yl, core),
        "z+": dev(x, yh, step(z, 1), yl, core), "z-": dev(x, yh, step(z, 3), yl, core),
        "ya": dev(x, yh, z, 1 - yl, core), "yb": dev(x, 1 - yh, z, 1 - yl, core),
        "mate": dev(x, yh, z, yl, 1 - core),
    }
    rows_of = [((row + i) % NROW, col) for i in range(1, NROW)]
    cols_of = [(row, (col + i) % NCOL) for i in range(1, NCOL)]

    barrier = pltpu.get_barrier_semaphore()
    greet = rows_of + cols_of + [peer["yb"]]
    for device in greet:
        pl.semaphore_signal(barrier, inc=1, device_id=device, device_id_type=MESH)

    tile = dens[...]
    dcol[row] = tile
    drow[col] = tile
    acc[...] = jnp.zeros_like(acc)
    nr, nc = ROWS // BLK, COLS // BLK
    rm = (lax.broadcasted_iota(jnp.int32, (nr, ROWS), 0)
          == lax.broadcasted_iota(jnp.int32, (nr, ROWS), 1) // BLK)
    cm = (lax.broadcasted_iota(jnp.int32, (COLS, nc), 1)
          == lax.broadcasted_iota(jnp.int32, (COLS, nc), 0) // BLK)
    part = jnp.dot(cm.astype(jnp.float32), pat[...].astype(jnp.float32),
                   preferred_element_type=jnp.float32)
    mask = jnp.dot(part, rm.astype(jnp.float32), preferred_element_type=jnp.float32)

    pl.semaphore_wait(barrier, len(greet))

    copies = {}

    def put(name, src, dst, device):
        i = len(copies)
        copies[name] = pltpu.make_async_remote_copy(
            src_ref=src, dst_ref=dst, send_sem=send.at[i], recv_sem=recv.at[i],
            device_id=device, device_id_type=MESH)
        copies[name].start()

    def wait(name):
        copies[name].wait_recv()

    rowslots = {
        "mine": row, "back": rowslot(step(x, 3), yh), "ahead": rowslot(step(x, 1), yh),
        "far": rowslot(step(x, 2), yh), "mine_p": rowslot(x, 1 - yh),
        "back_p": rowslot(step(x, 3), 1 - yh), "ahead_p": rowslot(step(x, 1), 1 - yh),
        "far_p": rowslot(step(x, 2), 1 - yh),
    }
    colslots = {
        "mine": col, "back": colslot(step(z, 3), yl), "ahead": colslot(step(z, 1), yl),
        "far": colslot(step(z, 2), yl), "mine_p": colslot(z, 1 - yl),
        "back_p": colslot(step(z, 3), 1 - yl), "ahead_p": colslot(step(z, 1), 1 - yl),
        "far_p": colslot(step(z, 2), 1 - yl),
    }

    def panel_copy(buf, slots):
        def make(name, link, src, dst, first, rows, i, p):
            ref = buf.at[slots[src], pl.ds(first, rows), :]
            return lambda _: put(name, ref, ref, peer[link])
        return make

    def column_copy(name, link, src, dst, first, rows, i, p):
        span = pl.ds(first, rows)
        here = dcol.at[rowslots[src], span, :]
        if link in ("x+", "x-"):
            return lambda _: put(name, here, here, peer[link])
        place = ("mine", "back", "ahead", "far").index(src)
        between = hop.at[place, span, :]
        if i == 0:
            return lambda _: put(name, here, between, peer[link])
        origin = rowslot(step(x, (0, 3, 1, 2)[place]), yh if link == "yb" else 1 - yh)
        there = dcol.at[origin, span, :]
        return lambda _: put(name, between, there, peer[link])

    def mates(plan, tag, buf, fills, pieces):
        given = {"mine": []}
        name = f"{tag}m"
        ref = buf.at[col]
        plan.add(name, "mate", COLS, [], lambda _, n=name, r=ref: put(n, r, r, peer["mate"]))
        given["mine"].append(name)
        for slot, by in fills.items():
            given[slot] = []
            groups = [q[:2] for q in pieces] if slot == "far_p" else GROUPS
            for first, rows in groups:
                deps = [by[p] for p, q in enumerate(pieces) if first <= q[0] < first + rows]
                name = f"{tag}m{slot}{first}"
                ref = buf.at[colslots[slot], pl.ds(first, rows), :]
                plan.add(name, "mate", rows, deps, lambda _, n=name, r=ref: put(n, r, r, peer["mate"]))
                given[slot].append(name)
        return {slot: list(by.values()) + given[slot] for slot, by in fills.items()} | {"mine": given["mine"]}

    def product(panel, k):
        acc[...] += dot3(dcol[k], panel[pl.ds(2 * k, 2)].reshape(2 * COLS, ROWS))

    def pick(i, values):
        k = values[-1]
        for j in reversed(range(len(values) - 1)):
            k = jnp.where(i == j, values[j], k)
        return k

    def products(panel, ks):
        def do(_):
            if len(ks) == 1:
                product(panel, ks[0])
                return

            def run(i, carry):
                product(panel, pick(i, ks))
                return carry

            lax.fori_loop(0, len(ks), run, 0)
        return do

    plan = Plan()
    fill_c = ring(plan, "C", PIECES_D, "x+", "x-",
                  lambda p: ("ya", "yb") if PIECES_D[p][3] > 0 else ("yb", "ya"), column_copy)
    fill_r = ring(plan, "R", PIECES_D, "z+", "z-", lambda p: ("ya",), panel_copy(drow, colslots))
    have = mates(plan, "R", drow, fill_r, PIECES_D)

    def need(r_slots, c_slots):
        return ([n for s in r_slots for n in have[s]] + [n for s in c_slots for n in fill_c[s].values()])

    d, even = (z - x + 4) % 4, yl == yh
    ny = 1 - yl
    o0 = jnp.where(d == 2, step(x, 1), x)
    o1 = jnp.where(d <= 1, step(x, 1), step(x, 3))
    o2 = jnp.where(d == 0, step(x, 3), step(z, 2))
    o3 = step(x, 2)
    sel = lambda a, b: jnp.where(even, a, b)
    stage1 = [rowslot(x, yl), sel(rowslot(step(x, 1), yl), rowslot(z, yh))]
    stage2 = [sel(rowslot(step(x, 2), yl), rowslot(step(x, 1), yl)), rowslot(step(x, 3), yl),
              sel(rowslot(o0, ny), rowslot(step(z, 1), yh)), sel(rowslot(o1, ny), rowslot(step(z, 3), yh))]
    stage3 = [sel(rowslot(o2, ny), rowslot(step(x, 2), yl)), sel(rowslot(o3, ny), rowslot(step(z, 2), yh))]
    near = ["back", "ahead", "far", "mine_p"]
    plan.add("work1", "work", 2.6, need(["mine"] + near, near), products(drow, stage1))
    near2 = near + ["back_p", "ahead_p"]
    plan.add("work2", "work", 5.2, need(near2, near2) + ["work1"], products(drow, stage2))
    near3 = near2 + ["far_p"]
    plan.add("work3", "work", 2.6, need(near3, near3) + ["work2"], products(drow, stage3))
    plan.run(wait)

    w8 = jnp.broadcast_to(wts[...][None, :], (8, ROWS))

    def column_sums(value):
        return lax.dot_general(w8, value, (((1,), (1,)), ((), ())),
                               precision=lax.Precision.HIGHEST, preferred_element_type=jnp.float32)

    srow[col] = mask * acc[...]

    plan = Plan()
    fill_s = ring(plan, "S", PIECES_S, "z+", "z-", lambda p: ("ya",), panel_copy(srow, colslots))
    have = mates(plan, "S", srow, fill_s, PIECES_S)

    def sums(_):
        first = lax.broadcasted_iota(jnp.int32, (8, COLS), 0) == 0
        value = jnp.where(first, column_sums(acc[...]), column_sums(srow[col]))
        acc[...] = jnp.zeros_like(acc)
        sums_out[...] = value
        sums_in[row] = value
        for i, device in enumerate(rows_of):
            put(f"sums{i}", sums_out, sums_in.at[row], device)

    def parts(_):
        for i in range(NROW - 1):
            wait(f"sums{i}")
        total = sums_in[0]
        for i in range(1, NROW):
            total += sums_in[i]
        chk[0:1, :] = total[0:1]

        def run(k, carry):
            value = dot3(total, dcol[k])
            parts_out[2 * k] = value[:, :COLS]
            parts_out[2 * k + 1] = value[:, COLS:]
            return carry

        lax.fori_loop(0, NROW, run, 0)
        parts_in[col] = parts_out[col]
        for i, device in enumerate(cols_of):
            put(f"parts{i}", parts_out.at[device[1]], parts_in.at[col], device)

    plan.add("sums", "work", 2.5, [], sums)
    plan.add("work0", "work", 1.3, have["mine"] + ["sums"], products(srow, [rowslot(z, yl)]))
    plan.add("parts", "work", 6.0, fill_s["far"].values(), parts)
    plan.add("work1", "work", 2.6, have["back"] + have["ahead"] + ["work0"],
             products(srow, [rowslot(step(z, 3), yl), rowslot(step(z, 1), yl)]))
    plan.add("work2", "work", 2.6, have["far"] + have["mine_p"] + ["work1"],
             products(srow, [rowslot(step(z, 2), yl), rowslot(z, 1 - yl)]))
    plan.add("work3", "work", 2.6, have["back_p"] + have["ahead_p"] + ["work2"],
             products(srow, [rowslot(step(z, 3), 1 - yl), rowslot(step(z, 1), 1 - yl)]))
    plan.add("work4", "work", 1.3, have["far_p"] + ["work3"],
             products(srow, [rowslot(step(z, 2), 1 - yl)]))
    plan.run(wait)

    out[...] = 3.0 * srow[col] - 2.0 * (mask * acc[...])
    for i in range(NCOL - 1):
        wait(f"parts{i}")
    total = parts_in[0]
    for i in range(1, NCOL):
        total += parts_in[i]
    chk[1:2, :] = total[1:2]
    for copy in copies.values():
        copy.wait_send()
    assert len(copies) <= SEMS, len(copies)


def body(density, pattern, weights):
    f32 = jnp.float32
    vmem = pl.BlockSpec(memory_space=pltpu.VMEM)
    purified, checks = pl.pallas_call(
        kernel,
        out_shape=(jax.ShapeDtypeStruct((COLS, ROWS), f32), jax.ShapeDtypeStruct((2, COLS), f32)),
        in_specs=[vmem] * 3,
        out_specs=(vmem, vmem),
        scratch_shapes=[
            pltpu.VMEM((NROW, COLS, ROWS), f32),
            pltpu.VMEM((NCOL, COLS, ROWS), f32),
            pltpu.VMEM((NCOL, COLS, ROWS), f32),
            pltpu.VMEM((4, COLS, ROWS), f32),
            pltpu.VMEM((COLS, ROWS), f32),
            pltpu.VMEM((8, COLS), f32),
            pltpu.VMEM((NROW, 8, COLS), f32),
            pltpu.VMEM((NCOL, 8, COLS), f32),
            pltpu.VMEM((NCOL, 8, COLS), f32),
            pltpu.SemaphoreType.DMA((SEMS,)),
            pltpu.SemaphoreType.DMA((SEMS,)),
        ],
        compiler_params=pltpu.CompilerParams(
            collective_id=0, has_side_effects=True, vmem_limit_bytes=63 * 1024 * 1024),
        name="purify",
    )(density.T, pattern.T, weights)
    return purified.T, checks


def solution(mesh):
    in_specs = (P("row", "col"), P("row", "col"), P("row"))
    out_specs = (P("row", "col"), P(None, "col"))
    return jax.shard_map(body, mesh=mesh, in_specs=in_specs, out_specs=out_specs, check_vma=False)
```

```python
import jax
import jax.numpy as jnp
from jax import lax
from jax.experimental import pallas as pl
from jax.experimental.pallas import tpu as pltpu
from jax.sharding import PartitionSpec as P

BLK = 64
MESH = pl.DeviceIdType.MESH
ROWS, COLS = 640, 320
NROW, NCOL = 8, 16
SEMS = 240

LINK_ROW, LINK_LATENCY = 0.0545, 1.7
MATE_ROW, MATE_LATENCY = 0.0057, 1.0
LEAD = 5.0

PIECES_C = ((0, 72, "first", 1), (72, 72, "first", 1), (144, 16, "after", 1),
            (160, 72, "first", -1), (232, 72, "first", -1), (304, 16, "after", -1))
PIECES_R = ((0, 64, "first", 1), (64, 72, "first", 1), (136, 24, "after", 1),
            (160, 64, "first", -1), (224, 72, "first", -1), (296, 24, "after", -1))
PIECES_S = ((0, 88, "first", 1), (88, 72, "after", 1), (160, 88, "first", -1), (248, 72, "after", -1))
GROUPS = ((0, 160), (160, 160))


class Plan:
    def __init__(self):
        self.items, self.made = {}, {}

    def add(self, name, link, rows, deps, do):
        if link == "work":
            length, latency = rows, 0.0
        elif link == "mate":
            length, latency = rows * MATE_ROW, MATE_LATENCY
        else:
            length, latency = rows * LINK_ROW, LINK_LATENCY
        self.items[name] = (link, length, latency, tuple(deps), do)

    def order(self):
        items = self.items
        after = {name: [] for name in items}
        for name, item in items.items():
            for dep in item[3]:
                after[dep].append(name)
        level = {}
        for name in reversed(list(items)):
            _, length, latency, _, _ = items[name]
            level[name] = length + latency + max([level[n] for n in after[name]], default=0.0)
        free, there, events = {}, {}, []
        left = list(items)
        while left:
            best = None
            for name in left:
                link, _, _, deps, _ = items[name]
                if all(dep in there for dep in deps):
                    ready = max([there[dep] for dep in deps], default=0.0)
                    key = (max(ready, free.get(link, 0.0)), -level[name], len(events))
                    if best is None or key < best[0]:
                        best = (key, name, ready)
            (start, _, _), name, ready = best
            link, length, latency, _, _ = items[name]
            free[link] = start + length
            there[name] = start + length + latency
            issue = start if link == "work" else max(ready, start - LEAD)
            events.append((issue, len(events), name))
            left.remove(name)
        return [name for _, _, name in sorted(events)], there

    def run(self, wait):
        done = set()
        for name in self.order()[0]:
            _, _, _, deps, do = self.items[name]
            for dep in deps:
                if dep not in done and self.items[dep][0] != "work":
                    wait(dep)
                    done.add(dep)
            do(name)
        for name in self.items:
            if name not in done and self.items[name][0] != "work":
                wait(name)


def ring(plan, tag, pieces, plus, minus, cross, send_to):
    fills = {slot: {} for slot in ("back", "ahead", "far", "mine_p", "back_p", "ahead_p", "far_p")}

    def over(name, src, dst, p, deps):
        first, rows = pieces[p][:2]
        last = deps
        for i, link in enumerate(cross(p)):
            step = f"{name}/{i}"
            plan.add(step, link, rows, last, send_to(step, link, src, dst, first, rows, i, p))
            last = [step]
        fills[dst][p] = last[0]
        return last

    def around(kind, p, deps, slots):
        mine, back, ahead, far = slots
        first, rows, _, way = pieces[p]
        names = {}
        for link, dst in ((plus, back), (minus, ahead)):
            name = f"{tag}{kind}{link}{p}"
            plan.add(name, link, rows, deps, send_to(name, link, mine, dst, first, rows, 0, p))
            fills[dst][p] = name
            names[link] = name
        link, src = (plus, back) if way > 0 else (minus, ahead)
        name = f"{tag}{kind}far{p}"
        plan.add(name, link, rows, [names[link]], send_to(name, link, src, far, first, rows, 0, p))
        fills[far][p] = name

    for p, (first, rows, when, way) in enumerate(pieces):
        around("own", p, [], ("mine", "back", "ahead", "far"))
        if when == "first":
            last = over(f"{tag}y{p}", "mine", "mine_p", p, [])
            around("par", p, last, ("mine_p", "back_p", "ahead_p", "far_p"))
        else:
            over(f"{tag}y{p}", "mine", "mine_p", p, [])
            for slot in ("back", "ahead", "far"):
                over(f"{tag}y{slot}{p}", slot, slot + "_p", p, [fills[slot][p]])
    return fills


def split(value):
    high = value.astype(jnp.bfloat16)
    low = (value - high.astype(jnp.float32)).astype(jnp.bfloat16)
    return high, low


def dot3(a, b):
    (a_hi, a_lo), (b_hi, b_lo) = split(a), split(b)
    dot = lambda u, v: jnp.dot(u, v, preferred_element_type=jnp.float32)
    return dot(a_hi, b_hi) + dot(a_hi, b_lo) + dot(a_lo, b_hi)


def kernel(dens, pat_in, wts_in, out, chk, dcol, drow, srow, hop, acc, pat, wts,
           sums_out, sums_in, parts_out, parts_in, load, send, recv):
    row, col = lax.axis_index("row"), lax.axis_index("col")
    x, yh = row // 2, row % 2
    z, yl, core = col // 4, (col // 2) % 2, col % 2

    def dev(x_, yh_, z_, yl_, core_):
        return (x_ * 2 + yh_, (z_ * 2 + yl_) * 2 + core_)

    def step(value, by):
        return (value + by) % 4

    def rowslot(x_, yh_):
        return x_ * 2 + yh_

    def colslot(z_, yl_):
        return (z_ * 2 + yl_) * 2 + core

    peer = {
        "x+": dev(step(x, 1), yh, z, yl, core), "x-": dev(step(x, 3), yh, z, yl, core),
        "z+": dev(x, yh, step(z, 1), yl, core), "z-": dev(x, yh, step(z, 3), yl, core),
        "ya": dev(x, yh, z, 1 - yl, core), "yb": dev(x, 1 - yh, z, 1 - yl, core),
        "mate": dev(x, yh, z, yl, 1 - core),
    }
    rows_of = [((row + i) % NROW, col) for i in range(1, NROW)]
    cols_of = [(row, (col + i) % NCOL) for i in range(1, NCOL)]

    barrier = pltpu.get_barrier_semaphore()
    greet = list(peer.values())
    for device in greet:
        pl.semaphore_signal(barrier, inc=1, device_id=device, device_id_type=MESH)
    loads = [pltpu.make_async_copy(src, dst, load.at[i]) for i, (src, dst) in enumerate((
        (pat_in, pat), (wts_in, wts), (dens, drow.at[col]), (dens, dcol.at[row])))]
    for copy in loads:
        copy.start()
    for copy in loads[:2]:
        copy.wait()

    acc[...] = jnp.zeros_like(acc)
    nr, nc = ROWS // BLK, COLS // BLK
    rm = (lax.broadcasted_iota(jnp.int32, (nr, ROWS), 0)
          == lax.broadcasted_iota(jnp.int32, (nr, ROWS), 1) // BLK)
    cm = (lax.broadcasted_iota(jnp.int32, (COLS, nc), 1)
          == lax.broadcasted_iota(jnp.int32, (COLS, nc), 0) // BLK)
    part = jnp.dot(cm.astype(jnp.float32), pat[...].astype(jnp.float32),
                   preferred_element_type=jnp.float32)
    mask = jnp.dot(part, rm.astype(jnp.float32), preferred_element_type=jnp.float32)

    for copy in loads[2:]:
        copy.wait()
    pl.semaphore_wait(barrier, len(greet))

    copies = {}

    def put(name, src, dst, device):
        i = len(copies)
        copies[name] = pltpu.make_async_remote_copy(
            src_ref=src, dst_ref=dst, send_sem=send.at[i], recv_sem=recv.at[i],
            device_id=device, device_id_type=MESH)
        copies[name].start()

    def wait(name):
        copies[name].wait_recv()

    rowslots = {
        "mine": row, "back": rowslot(step(x, 3), yh), "ahead": rowslot(step(x, 1), yh),
        "far": rowslot(step(x, 2), yh), "mine_p": rowslot(x, 1 - yh),
        "back_p": rowslot(step(x, 3), 1 - yh), "ahead_p": rowslot(step(x, 1), 1 - yh),
        "far_p": rowslot(step(x, 2), 1 - yh),
    }
    colslots = {
        "mine": col, "back": colslot(step(z, 3), yl), "ahead": colslot(step(z, 1), yl),
        "far": colslot(step(z, 2), yl), "mine_p": colslot(z, 1 - yl),
        "back_p": colslot(step(z, 3), 1 - yl), "ahead_p": colslot(step(z, 1), 1 - yl),
        "far_p": colslot(step(z, 2), 1 - yl),
    }

    def panel_copy(buf, slots):
        def make(name, link, src, dst, first, rows, i, p):
            ref = buf.at[slots[src], pl.ds(first, rows), :]
            return lambda _: put(name, ref, ref, peer[link])
        return make

    def column_copy(name, link, src, dst, first, rows, i, p):
        span = pl.ds(first, rows)
        here = dcol.at[rowslots[src], span, :]
        if link in ("x+", "x-"):
            return lambda _: put(name, here, here, peer[link])
        place = ("mine", "back", "ahead", "far").index(src)
        between = hop.at[place, span, :]
        if i == 0:
            return lambda _: put(name, here, between, peer[link])
        origin = rowslot(step(x, (0, 3, 1, 2)[place]), yh if link == "yb" else 1 - yh)
        there = dcol.at[origin, span, :]
        return lambda _: put(name, between, there, peer[link])

    def mates(plan, tag, buf, fills, pieces):
        given = {"mine": []}
        name = f"{tag}m"
        ref = buf.at[col]
        plan.add(name, "mate", COLS, [], lambda _, n=name, r=ref: put(n, r, r, peer["mate"]))
        given["mine"].append(name)
        for slot, by in fills.items():
            given[slot] = []
            groups = [q[:2] for q in pieces] if slot == "far_p" else GROUPS
            for first, rows in groups:
                deps = [by[p] for p, q in enumerate(pieces) if first <= q[0] < first + rows]
                name = f"{tag}m{slot}{first}"
                ref = buf.at[colslots[slot], pl.ds(first, rows), :]
                plan.add(name, "mate", rows, deps, lambda _, n=name, r=ref: put(n, r, r, peer["mate"]))
                given[slot].append(name)
        return {slot: list(by.values()) + given[slot] for slot, by in fills.items()} | {"mine": given["mine"]}

    def product(panel, k):
        acc[...] += dot3(dcol[k], panel[pl.ds(2 * k, 2)].reshape(2 * COLS, ROWS))

    def pick(i, values):
        k = values[-1]
        for j in reversed(range(len(values) - 1)):
            k = jnp.where(i == j, values[j], k)
        return k

    def products(panel, ks):
        def do(_):
            if len(ks) == 1:
                product(panel, ks[0])
                return

            def run(i, carry):
                product(panel, pick(i, ks))
                return carry

            lax.fori_loop(0, len(ks), run, 0)
        return do

    plan = Plan()
    fill_c = ring(plan, "C", PIECES_C, "x+", "x-",
                  lambda p: ("ya", "yb") if PIECES_C[p][3] > 0 else ("yb", "ya"), column_copy)
    fill_r = ring(plan, "R", PIECES_R, "z+", "z-", lambda p: ("ya",), panel_copy(drow, colslots))
    have = mates(plan, "R", drow, fill_r, PIECES_R)

    def need(r_slots, c_slots):
        return ([n for s in r_slots for n in have[s]] + [n for s in c_slots for n in fill_c[s].values()])

    d, even = (z - x + 4) % 4, yl == yh
    ny = 1 - yl
    o0 = jnp.where(d == 2, step(x, 1), x)
    o1 = jnp.where(d <= 1, step(x, 1), step(x, 3))
    o2 = jnp.where(d == 0, step(x, 3), step(z, 2))
    o3 = step(x, 2)
    sel = lambda a, b: jnp.where(even, a, b)
    stage1 = [rowslot(x, yl), sel(rowslot(step(x, 1), yl), rowslot(z, yh))]
    stage2 = [sel(rowslot(step(x, 2), yl), rowslot(step(x, 1), yl)), rowslot(step(x, 3), yl),
              sel(rowslot(o0, ny), rowslot(step(z, 1), yh)), sel(rowslot(o1, ny), rowslot(step(z, 3), yh))]
    stage3 = [sel(rowslot(o2, ny), rowslot(step(x, 2), yl)), sel(rowslot(o3, ny), rowslot(step(z, 2), yh))]
    near = ["back", "ahead", "far", "mine_p"]
    plan.add("work1", "work", 2.6, need(["mine"] + near, near), products(drow, stage1))
    near2 = near + ["back_p", "ahead_p"]
    plan.add("work2", "work", 5.2, need(near2, near2) + ["work1"], products(drow, stage2))
    near3 = near2 + ["far_p"]
    plan.add("work3", "work", 2.6, need(near3, near3) + ["work2"], products(drow, stage3))
    plan.run(wait)

    w_col = jnp.broadcast_to(wts[...][None, :], (128, ROWS)).T

    def column_sums(value):
        return dot3(value, w_col).T[:8]

    srow[col] = mask * acc[...]

    plan = Plan()
    fill_s = ring(plan, "S", PIECES_S, "z+", "z-", lambda p: ("ya",), panel_copy(srow, colslots))
    have = mates(plan, "S", srow, fill_s, PIECES_S)

    def sums(_):
        first = lax.broadcasted_iota(jnp.int32, (8, COLS), 0) == 0
        value = jnp.where(first, column_sums(acc[...]), column_sums(srow[col]))
        acc[...] = jnp.zeros_like(acc)
        sums_out[0] = value
        sums_in[row] = value
        for i, device in enumerate(rows_of):
            put(f"sums{i}", sums_out.at[0], sums_in.at[row], device)

    def total_sums(_):
        for i in range(NROW - 1):
            wait(f"sums{i}")
        total = sums_in[0]
        for i in range(1, NROW):
            total += sums_in[i]
        chk[0:1, :] = total[0:1]
        sums_out[1] = total

    def parts(first):
        def do(_):
            def run(k, carry):
                value = dot3(sums_out[1], dcol[k])
                parts_out[2 * k] = value[:, :COLS]
                parts_out[2 * k + 1] = value[:, COLS:]
                return carry

            lax.fori_loop(first, first + 2, run, 0)
        return do

    def spread(_):
        parts_in[col] = parts_out[col]
        for i, device in enumerate(cols_of):
            put(f"parts{i}", parts_out.at[device[1]], parts_in.at[col], device)

    plan.add("sums", "work", 2.5, [], sums)
    plan.add("work0", "work", 1.3, have["mine"] + ["sums"], products(srow, [rowslot(z, yl)]))
    plan.add("total", "work", 0.3, list(fill_s["back"].values()) + ["work0"], total_sums)
    for k in range(0, NROW, 2):
        plan.add(f"parts{k}", "work", 2.0, ["total" if k == 0 else f"parts{k - 2}"], parts(k))
    plan.add("spread", "work", 0.3, ["parts6"], spread)
    plan.add("work1", "work", 2.6, have["back"] + have["ahead"] + ["work0"],
             products(srow, [rowslot(step(z, 3), yl), rowslot(step(z, 1), yl)]))
    plan.add("work2", "work", 2.6, have["far"] + have["mine_p"] + ["work1"],
             products(srow, [rowslot(step(z, 2), yl), rowslot(z, 1 - yl)]))
    plan.add("work3", "work", 2.6, have["back_p"] + have["ahead_p"] + ["work2"],
             products(srow, [rowslot(step(z, 3), 1 - yl), rowslot(step(z, 1), 1 - yl)]))
    plan.add("work4", "work", 1.3, have["far_p"] + ["work3"],
             products(srow, [rowslot(step(z, 2), 1 - yl)]))
    plan.run(wait)

    out[...] = 3.0 * srow[col] - 2.0 * (mask * acc[...])
    for i in range(NCOL - 1):
        wait(f"parts{i}")
    total = parts_in[0]
    for i in range(1, NCOL):
        total += parts_in[i]
    chk[1:2, :] = total[1:2]
    for copy in copies.values():
        copy.wait_send()
    assert len(copies) <= SEMS, len(copies)


def body(density, pattern, weights):
    f32 = jnp.float32
    vmem = pl.BlockSpec(memory_space=pltpu.VMEM)
    hbm = pl.BlockSpec(memory_space=pltpu.HBM)
    purified, checks = pl.pallas_call(
        kernel,
        out_shape=(jax.ShapeDtypeStruct((COLS, ROWS), f32), jax.ShapeDtypeStruct((2, COLS), f32)),
        in_specs=[hbm] * 3,
        out_specs=(vmem, vmem),
        scratch_shapes=[
            pltpu.VMEM((NROW, COLS, ROWS), f32),
            pltpu.VMEM((NCOL, COLS, ROWS), f32),
            pltpu.VMEM((NCOL, COLS, ROWS), f32),
            pltpu.VMEM((4, COLS, ROWS), f32),
            pltpu.VMEM((COLS, ROWS), f32),
            pltpu.VMEM((COLS // BLK, ROWS // BLK), jnp.int32),
            pltpu.VMEM((ROWS,), f32),
            pltpu.VMEM((2, 8, COLS), f32),
            pltpu.VMEM((NROW, 8, COLS), f32),
            pltpu.VMEM((NCOL, 8, COLS), f32),
            pltpu.VMEM((NCOL, 8, COLS), f32),
            pltpu.SemaphoreType.DMA((4,)),
            pltpu.SemaphoreType.DMA((SEMS,)),
            pltpu.SemaphoreType.DMA((SEMS,)),
        ],
        compiler_params=pltpu.CompilerParams(
            collective_id=0, has_side_effects=True, vmem_limit_bytes=46 * 1024 * 1024),
        name="purify",
    )(*(pltpu.with_memory_space_constraint(a, pltpu.HBM) for a in (density.T, pattern.T, weights)))
    return purified.T, checks


def solution(mesh):
    in_specs = (P("row", "col"), P("row", "col"), P("row"))
    out_specs = (P("row", "col"), P(None, "col"))
    return jax.shard_map(body, mesh=mesh, in_specs=in_specs, out_specs=out_specs, check_vma=False)
```

```python
import jax
import jax.numpy as jnp
from jax import lax
from jax.experimental import pallas as pl
from jax.experimental.pallas import tpu as pltpu
from jax.sharding import PartitionSpec as P

BLK = 64
MESH = pl.DeviceIdType.MESH
ROWS, COLS = 640, 320
NROW, NCOL = 8, 16
SEMS = 240

LINK_ROW, LINK_LATENCY = 0.0545, 1.7
MATE_ROW, MATE_LATENCY = 0.0057, 1.0
LEAD, PATIENCE, ISSUE = 3.0, 0.5, 0.02

PIECES_C = ((0, 72, "first", 1), (72, 72, "first", 1), (144, 16, "after", 1),
            (160, 72, "first", -1), (232, 72, "first", -1), (304, 16, "after", -1))
PIECES_R = ((0, 64, "first", 1), (64, 72, "first", 1), (136, 24, "after", 1),
            (160, 64, "first", -1), (224, 72, "first", -1), (296, 24, "after", -1))
PIECES_S = ((0, 88, "first", 1), (88, 72, "after", 1), (160, 88, "first", -1), (248, 72, "after", -1))
GROUPS = ((0, 160), (160, 160))


class Plan:
    def __init__(self):
        self.items, self.made = {}, {}

    def add(self, name, link, rows, deps, do):
        if link == "work":
            length, latency = rows, 0.0
        elif link == "mate":
            length, latency = rows * MATE_ROW, MATE_LATENCY
        else:
            length, latency = rows * LINK_ROW, LINK_LATENCY
        self.items[name] = (link, length, latency, tuple(deps), do)

    def order(self):
        items = self.items
        after = {name: [] for name in items}
        for name, item in items.items():
            for dep in item[3]:
                after[dep].append(name)
        level = {}
        for name in reversed(list(items)):
            _, length, latency, _, _ = items[name]
            level[name] = length + latency + max([level[n] for n in after[name]], default=0.0)
        now, free, there, program = 0.0, {}, {}, []
        left = sorted(items, key=lambda name: -level[name])
        while left:
            ready = {}
            for name in left:
                deps = items[name][3]
                if all(dep in there for dep in deps):
                    ready[name] = max([there[dep] for dep in deps], default=0.0)
            chosen, following = None, []
            for name, since in ready.items():
                link = items[name][0]
                if link == "work":
                    if since > now:
                        following.append(since)
                    continue
                since = max(since, free.get(link, 0.0) - LEAD)
                if since <= now:
                    chosen = name
                    break
                following.append(since)
            if chosen is None:
                for name, since in ready.items():
                    link, length = items[name][:2]
                    if link != "work" or since > now:
                        continue
                    idle = max([now + length - max(free.get(items[n][0], 0.0), t)
                                for n, t in ready.items() if items[n][0] not in ("work", "mate")],
                               default=0.0)
                    if idle <= PATIENCE:
                        chosen = name
                        break
            if chosen is None:
                if following:
                    now = min(following)
                    continue
                chosen = next(iter(ready))
            link, length, latency, _, _ = items[chosen]
            if link == "work":
                now += length
                there[chosen] = now
            else:
                free[link] = max(now, free.get(link, 0.0)) + length
                there[chosen] = free[link] + latency
                now += ISSUE
            program.append(chosen)
            left.remove(chosen)
        return program, there

    def run(self, wait):
        done = set()
        for name in self.order()[0]:
            _, _, _, deps, do = self.items[name]
            for dep in deps:
                if dep not in done and self.items[dep][0] != "work":
                    wait(dep)
                    done.add(dep)
            do(name)
        for name in self.items:
            if name not in done and self.items[name][0] != "work":
                wait(name)


def ring(plan, tag, pieces, plus, minus, cross, send_to):
    fills = {slot: {} for slot in ("back", "ahead", "far", "mine_p", "back_p", "ahead_p", "far_p")}

    def over(name, src, dst, p, deps):
        first, rows = pieces[p][:2]
        last = deps
        for i, link in enumerate(cross(p)):
            step = f"{name}/{i}"
            plan.add(step, link, rows, last, send_to(step, link, src, dst, first, rows, i, p))
            last = [step]
        fills[dst][p] = last[0]
        return last

    def around(kind, p, deps, slots):
        mine, back, ahead, far = slots
        first, rows, _, way = pieces[p]
        names = {}
        for link, dst in ((plus, back), (minus, ahead)):
            name = f"{tag}{kind}{link}{p}"
            plan.add(name, link, rows, deps, send_to(name, link, mine, dst, first, rows, 0, p))
            fills[dst][p] = name
            names[link] = name
        link, src = (plus, back) if way > 0 else (minus, ahead)
        name = f"{tag}{kind}far{p}"
        plan.add(name, link, rows, [names[link]], send_to(name, link, src, far, first, rows, 0, p))
        fills[far][p] = name

    for p, (first, rows, when, way) in enumerate(pieces):
        around("own", p, [], ("mine", "back", "ahead", "far"))
        if when == "first":
            last = over(f"{tag}y{p}", "mine", "mine_p", p, [])
            around("par", p, last, ("mine_p", "back_p", "ahead_p", "far_p"))
        else:
            over(f"{tag}y{p}", "mine", "mine_p", p, [])
            for slot in ("back", "ahead", "far"):
                over(f"{tag}y{slot}{p}", slot, slot + "_p", p, [fills[slot][p]])
    return fills


def split(value):
    high = value.astype(jnp.bfloat16)
    low = (value - high.astype(jnp.float32)).astype(jnp.bfloat16)
    return high, low


def dot3(a, b):
    (a_hi, a_lo), (b_hi, b_lo) = split(a), split(b)
    dot = lambda u, v: jnp.dot(u, v, preferred_element_type=jnp.float32)
    return dot(a_hi, b_hi) + dot(a_hi, b_lo) + dot(a_lo, b_hi)


def kernel(dens, pat_in, wts_in, out, chk, dcol, drow, srow, hop, acc, pat, wts,
           sums_out, sums_in, parts_out, parts_in, load, send, recv):
    row, col = lax.axis_index("row"), lax.axis_index("col")
    x, yh = row // 2, row % 2
    z, yl, core = col // 4, (col // 2) % 2, col % 2

    def dev(x_, yh_, z_, yl_, core_):
        return (x_ * 2 + yh_, (z_ * 2 + yl_) * 2 + core_)

    def step(value, by):
        return (value + by) % 4

    def rowslot(x_, yh_):
        return x_ * 2 + yh_

    def colslot(z_, yl_):
        return (z_ * 2 + yl_) * 2 + core

    peer = {
        "x+": dev(step(x, 1), yh, z, yl, core), "x-": dev(step(x, 3), yh, z, yl, core),
        "z+": dev(x, yh, step(z, 1), yl, core), "z-": dev(x, yh, step(z, 3), yl, core),
        "ya": dev(x, yh, z, 1 - yl, core), "yb": dev(x, 1 - yh, z, 1 - yl, core),
        "mate": dev(x, yh, z, yl, 1 - core),
    }
    rows_of = [((row + i) % NROW, col) for i in range(1, NROW)]
    cols_of = [(row, (col + i) % NCOL) for i in range(1, NCOL)]

    barrier = pltpu.get_barrier_semaphore()
    greet = list(peer.values())
    for device in greet:
        pl.semaphore_signal(barrier, inc=1, device_id=device, device_id_type=MESH)
    loads = [pltpu.make_async_copy(src, dst, load.at[i]) for i, (src, dst) in enumerate((
        (pat_in, pat), (wts_in, wts), (dens, drow.at[col]), (dens, dcol.at[row])))]
    for copy in loads:
        copy.start()
    for copy in loads[:2]:
        copy.wait()

    acc[...] = jnp.zeros_like(acc)
    nr, nc = ROWS // BLK, COLS // BLK
    rm = (lax.broadcasted_iota(jnp.int32, (nr, ROWS), 0)
          == lax.broadcasted_iota(jnp.int32, (nr, ROWS), 1) // BLK)
    cm = (lax.broadcasted_iota(jnp.int32, (COLS, nc), 1)
          == lax.broadcasted_iota(jnp.int32, (COLS, nc), 0) // BLK)
    part = jnp.dot(cm.astype(jnp.float32), pat[...].astype(jnp.float32),
                   preferred_element_type=jnp.float32)
    mask = jnp.dot(part, rm.astype(jnp.float32), preferred_element_type=jnp.float32)

    for copy in loads[2:]:
        copy.wait()
    pl.semaphore_wait(barrier, len(greet))

    copies = {}

    def put(name, src, dst, device):
        i = len(copies)
        copies[name] = pltpu.make_async_remote_copy(
            src_ref=src, dst_ref=dst, send_sem=send.at[i], recv_sem=recv.at[i],
            device_id=device, device_id_type=MESH)
        copies[name].start()

    def wait(name):
        copies[name].wait_recv()

    rowslots = {
        "mine": row, "back": rowslot(step(x, 3), yh), "ahead": rowslot(step(x, 1), yh),
        "far": rowslot(step(x, 2), yh), "mine_p": rowslot(x, 1 - yh),
        "back_p": rowslot(step(x, 3), 1 - yh), "ahead_p": rowslot(step(x, 1), 1 - yh),
        "far_p": rowslot(step(x, 2), 1 - yh),
    }
    colslots = {
        "mine": col, "back": colslot(step(z, 3), yl), "ahead": colslot(step(z, 1), yl),
        "far": colslot(step(z, 2), yl), "mine_p": colslot(z, 1 - yl),
        "back_p": colslot(step(z, 3), 1 - yl), "ahead_p": colslot(step(z, 1), 1 - yl),
        "far_p": colslot(step(z, 2), 1 - yl),
    }

    def panel_copy(buf, slots):
        def make(name, link, src, dst, first, rows, i, p):
            ref = buf.at[slots[src], pl.ds(first, rows), :]
            return lambda _: put(name, ref, ref, peer[link])
        return make

    def column_copy(name, link, src, dst, first, rows, i, p):
        span = pl.ds(first, rows)
        here = dcol.at[rowslots[src], span, :]
        if link in ("x+", "x-"):
            return lambda _: put(name, here, here, peer[link])
        place = ("mine", "back", "ahead", "far").index(src)
        between = hop.at[place, span, :]
        if i == 0:
            return lambda _: put(name, here, between, peer[link])
        origin = rowslot(step(x, (0, 3, 1, 2)[place]), yh if link == "yb" else 1 - yh)
        there = dcol.at[origin, span, :]
        return lambda _: put(name, between, there, peer[link])

    def mates(plan, tag, buf, fills, pieces):
        given = {"mine": []}
        name = f"{tag}m"
        ref = buf.at[col]
        plan.add(name, "mate", COLS, [], lambda _, n=name, r=ref: put(n, r, r, peer["mate"]))
        given["mine"].append(name)
        for slot, by in fills.items():
            given[slot] = []
            groups = [q[:2] for q in pieces] if slot == "far_p" else GROUPS
            for first, rows in groups:
                deps = [by[p] for p, q in enumerate(pieces) if first <= q[0] < first + rows]
                name = f"{tag}m{slot}{first}"
                ref = buf.at[colslots[slot], pl.ds(first, rows), :]
                plan.add(name, "mate", rows, deps, lambda _, n=name, r=ref: put(n, r, r, peer["mate"]))
                given[slot].append(name)
        return {slot: list(by.values()) + given[slot] for slot, by in fills.items()} | {"mine": given["mine"]}

    def product(panel, k):
        acc[...] += dot3(dcol[k], panel[pl.ds(2 * k, 2)].reshape(2 * COLS, ROWS))

    def pick(i, values):
        k = values[-1]
        for j in reversed(range(len(values) - 1)):
            k = jnp.where(i == j, values[j], k)
        return k

    def products(panel, ks):
        def do(_):
            if len(ks) == 1:
                product(panel, ks[0])
                return

            def run(i, carry):
                product(panel, pick(i, ks))
                return carry

            lax.fori_loop(0, len(ks), run, 0)
        return do

    plan = Plan()
    fill_c = ring(plan, "C", PIECES_C, "x+", "x-",
                  lambda p: ("ya", "yb") if PIECES_C[p][3] > 0 else ("yb", "ya"), column_copy)
    fill_r = ring(plan, "R", PIECES_R, "z+", "z-", lambda p: ("ya",), panel_copy(drow, colslots))
    have = mates(plan, "R", drow, fill_r, PIECES_R)

    def need(r_slots, c_slots):
        return ([n for s in r_slots for n in have[s]] + [n for s in c_slots for n in fill_c[s].values()])

    d, even = (z - x + 4) % 4, yl == yh
    ny = 1 - yl
    o0 = jnp.where(d == 2, step(x, 1), x)
    o1 = jnp.where(d <= 1, step(x, 1), step(x, 3))
    o2 = jnp.where(d == 0, step(x, 3), step(z, 2))
    o3 = step(x, 2)
    sel = lambda a, b: jnp.where(even, a, b)
    stage1 = [rowslot(x, yl), sel(rowslot(step(x, 1), yl), rowslot(z, yh))]
    stage2 = [sel(rowslot(step(x, 2), yl), rowslot(step(x, 1), yl)), rowslot(step(x, 3), yl),
              sel(rowslot(o0, ny), rowslot(step(z, 1), yh)), sel(rowslot(o1, ny), rowslot(step(z, 3), yh))]
    stage3 = [sel(rowslot(o2, ny), rowslot(step(x, 2), yl)), sel(rowslot(o3, ny), rowslot(step(z, 2), yh))]
    own, par = ["back", "ahead", "far"], ["mine_p", "back_p", "ahead_p"]
    needs = (
        (["mine"] + own, ["mine_p"]), (["mine"] + own + ["mine_p"], own),
        (["mine"] + own, ["far", "ahead_p"]), (["mine"] + own, ["back", "back_p"]),
        (par, own + ["mine_p", "ahead_p"]), (par, own + ["ahead_p", "back_p"]),
        (["mine"] + own + par + ["far_p"], own + par + ["far_p"]), ([], []),
    )
    deps = []
    for i, (k, slots) in enumerate(zip(stage1 + stage2 + stage3, needs)):
        deps = deps + need(*slots)
        plan.add(f"work{i}", "work", 1.3, deps + [f"work{j}" for j in range(i)], products(drow, [k]))
    plan.run(wait)

    w_col = jnp.broadcast_to(wts[...][None, :], (128, ROWS)).T

    def column_sums(value):
        return dot3(value, w_col).T[:8]

    srow[col] = mask * acc[...]

    plan = Plan()
    fill_s = ring(plan, "S", PIECES_S, "z+", "z-", lambda p: ("ya",), panel_copy(srow, colslots))
    have = mates(plan, "S", srow, fill_s, PIECES_S)

    def sums(_):
        first = lax.broadcasted_iota(jnp.int32, (8, COLS), 0) == 0
        value = jnp.where(first, column_sums(acc[...]), column_sums(srow[col]))
        acc[...] = jnp.zeros_like(acc)
        sums_out[0] = value
        sums_in[row] = value
        for i, device in enumerate(rows_of):
            put(f"sums{i}", sums_out.at[0], sums_in.at[row], device)

    def total_sums(_):
        for i in range(NROW - 1):
            wait(f"sums{i}")
        total = sums_in[0]
        for i in range(1, NROW):
            total += sums_in[i]
        chk[0:1, :] = total[0:1]
        sums_out[1] = total

    def parts(first):
        def do(_):
            def run(k, carry):
                value = dot3(sums_out[1], dcol[k])
                parts_out[2 * k] = value[:, :COLS]
                parts_out[2 * k + 1] = value[:, COLS:]
                return carry

            lax.fori_loop(first, first + 2, run, 0)
        return do

    def spread(_):
        parts_in[col] = parts_out[col]
        for i, device in enumerate(cols_of):
            put(f"parts{i}", parts_out.at[device[1]], parts_in.at[col], device)

    plan.add("sums", "work", 2.0, [], sums)
    plan.add("total", "work", 0.3, list(fill_s["back"].values()) + ["sums"], total_sums)
    for k in range(0, NROW, 2):
        plan.add(f"parts{k}", "work", 1.6, ["total" if k == 0 else f"parts{k - 2}"], parts(k))
    plan.add("spread", "work", 0.3, ["parts6"], spread)
    blocks = {"mine": (0, yl), "back": (3, yl), "ahead": (1, yl), "far": (2, yl)}
    blocks |= {f"{slot}_p": (by, 1 - y) for slot, (by, y) in blocks.items()}
    for slot, (by, y) in blocks.items():
        plan.add(f"work_{slot}", "work", 1.3, have[slot] + ["sums"],
                 products(srow, [rowslot(step(z, by), y)]))
    plan.run(wait)

    out[...] = 3.0 * srow[col] - 2.0 * (mask * acc[...])
    for i in range(NCOL - 1):
        wait(f"parts{i}")
    total = parts_in[0]
    for i in range(1, NCOL):
        total += parts_in[i]
    chk[1:2, :] = total[1:2]
    for copy in copies.values():
        copy.wait_send()
    assert len(copies) <= SEMS, len(copies)


def body(density, pattern, weights):
    f32 = jnp.float32
    vmem = pl.BlockSpec(memory_space=pltpu.VMEM)
    hbm = pl.BlockSpec(memory_space=pltpu.HBM)
    purified, checks = pl.pallas_call(
        kernel,
        out_shape=(jax.ShapeDtypeStruct((COLS, ROWS), f32), jax.ShapeDtypeStruct((2, COLS), f32)),
        in_specs=[hbm] * 3,
        out_specs=(vmem, vmem),
        scratch_shapes=[
            pltpu.VMEM((NROW, COLS, ROWS), f32),
            pltpu.VMEM((NCOL, COLS, ROWS), f32),
            pltpu.VMEM((NCOL, COLS, ROWS), f32),
            pltpu.VMEM((4, COLS, ROWS), f32),
            pltpu.VMEM((COLS, ROWS), f32),
            pltpu.VMEM((COLS // BLK, ROWS // BLK), jnp.int32),
            pltpu.VMEM((ROWS,), f32),
            pltpu.VMEM((2, 8, COLS), f32),
            pltpu.VMEM((NROW, 8, COLS), f32),
            pltpu.VMEM((NCOL, 8, COLS), f32),
            pltpu.VMEM((NCOL, 8, COLS), f32),
            pltpu.SemaphoreType.DMA((4,)),
            pltpu.SemaphoreType.DMA((SEMS,)),
            pltpu.SemaphoreType.DMA((SEMS,)),
        ],
        compiler_params=pltpu.CompilerParams(
            collective_id=0, has_side_effects=True, vmem_limit_bytes=46 * 1024 * 1024),
        name="purify",
    )(*(pltpu.with_memory_space_constraint(a, pltpu.HBM) for a in (density.T, pattern.T, weights)))
    return purified.T, checks


def solution(mesh):
    in_specs = (P("row", "col"), P("row", "col"), P("row"))
    out_specs = (P("row", "col"), P(None, "col"))
    return jax.shard_map(body, mesh=mesh, in_specs=in_specs, out_specs=out_specs, check_vma=False)
```

```python
import jax
import jax.numpy as jnp
from jax import lax
from jax.experimental import pallas as pl
from jax.experimental.pallas import tpu as pltpu
from jax.sharding import PartitionSpec as P

BLK = 64
MESH = pl.DeviceIdType.MESH
ROWS, COLS = 640, 320
NROW, NCOL = 8, 16
SEMS = 240

LINK_ROW, LINK_LATENCY = 0.0545, 3.0
MATE_ROW, MATE_LATENCY = 0.0057, 1.0
LEAD, PATIENCE, ISSUE = 3.0, 0.5, 0.02

PIECES_C = ((0, 72, "first", 1), (72, 72, "first", 1), (144, 16, "after", 1),
            (160, 72, "first", -1), (232, 72, "first", -1), (304, 16, "after", -1))
PIECES_R = ((0, 64, "first", 1), (64, 72, "first", 1), (136, 24, "after", 1),
            (160, 64, "first", -1), (224, 72, "first", -1), (296, 24, "after", -1))
PIECES_S = ((0, 88, "first", 1), (88, 72, "after", 1), (160, 88, "first", -1), (248, 72, "after", -1))
GROUPS = ((0, 160), (160, 160))


class Plan:
    def __init__(self):
        self.items, self.made = {}, {}

    def add(self, name, link, rows, deps, do):
        if link == "work":
            length, latency = rows, 0.0
        elif link == "mate":
            length, latency = rows * MATE_ROW, MATE_LATENCY
        else:
            length, latency = rows * LINK_ROW, LINK_LATENCY
        self.items[name] = (link, length, latency, tuple(deps), do)

    def order(self):
        items = self.items
        after = {name: [] for name in items}
        for name, item in items.items():
            for dep in item[3]:
                after[dep].append(name)
        level = {}
        for name in reversed(list(items)):
            _, length, latency, _, _ = items[name]
            level[name] = length + latency + max([level[n] for n in after[name]], default=0.0)
        now, free, there, program = 0.0, {}, {}, []
        left = sorted(items, key=lambda name: -level[name])
        while left:
            ready = {}
            for name in left:
                deps = items[name][3]
                if all(dep in there for dep in deps):
                    ready[name] = max([there[dep] for dep in deps], default=0.0)
            chosen, following = None, []
            for name, since in ready.items():
                link = items[name][0]
                if link == "work":
                    if since > now:
                        following.append(since)
                    continue
                since = max(since, free.get(link, 0.0) - LEAD)
                if since <= now:
                    chosen = name
                    break
                following.append(since)
            if chosen is None:
                for name, since in ready.items():
                    link, length = items[name][:2]
                    if link != "work" or since > now:
                        continue
                    idle = max([now + length - max(free.get(items[n][0], 0.0), t)
                                for n, t in ready.items() if items[n][0] not in ("work", "mate")],
                               default=0.0)
                    if idle <= PATIENCE:
                        chosen = name
                        break
            if chosen is None:
                if following:
                    now = min(following)
                    continue
                chosen = next(iter(ready))
            link, length, latency, _, _ = items[chosen]
            if link == "work":
                now += length
                there[chosen] = now
            else:
                free[link] = max(now, free.get(link, 0.0)) + length
                there[chosen] = free[link] + latency
                now += ISSUE
            program.append(chosen)
            left.remove(chosen)
        return program, there

    def run(self, wait):
        done = set()
        for name in self.order()[0]:
            _, _, _, deps, do = self.items[name]
            for dep in deps:
                if dep not in done and self.items[dep][0] != "work":
                    wait(dep)
                    done.add(dep)
            do(name)
        for name in self.items:
            if name not in done and self.items[name][0] != "work":
                wait(name)


def ring(plan, tag, pieces, plus, minus, cross, send_to, start=lambda p: []):
    fills = {slot: {} for slot in ("back", "ahead", "far", "mine_p", "back_p", "ahead_p", "far_p")}

    def over(name, src, dst, p, deps):
        first, rows = pieces[p][:2]
        last = deps
        for i, link in enumerate(cross(p)):
            step = f"{name}/{i}"
            plan.add(step, link, rows, last, send_to(step, link, src, dst, first, rows, i, p))
            last = [step]
        fills[dst][p] = last[0]
        return last

    def around(kind, p, deps, slots):
        mine, back, ahead, far = slots
        first, rows, _, way = pieces[p]
        names = {}
        for link, dst in ((plus, back), (minus, ahead)):
            name = f"{tag}{kind}{link}{p}"
            plan.add(name, link, rows, deps, send_to(name, link, mine, dst, first, rows, 0, p))
            fills[dst][p] = name
            names[link] = name
        link, src = (plus, back) if way > 0 else (minus, ahead)
        name = f"{tag}{kind}far{p}"
        plan.add(name, link, rows, [names[link]], send_to(name, link, src, far, first, rows, 0, p))
        fills[far][p] = name

    for p, (first, rows, when, way) in enumerate(pieces):
        around("own", p, start(p), ("mine", "back", "ahead", "far"))
        if when == "first":
            last = over(f"{tag}y{p}", "mine", "mine_p", p, start(p))
            around("par", p, last, ("mine_p", "back_p", "ahead_p", "far_p"))
        else:
            over(f"{tag}y{p}", "mine", "mine_p", p, start(p))
            for slot in ("back", "ahead", "far"):
                over(f"{tag}y{slot}{p}", slot, slot + "_p", p, [fills[slot][p]])
    return fills


def split(value):
    high = value.astype(jnp.bfloat16)
    low = (value - high.astype(jnp.float32)).astype(jnp.bfloat16)
    return high, low


def dot3(a, b):
    (a_hi, a_lo), (b_hi, b_lo) = split(a), split(b)
    dot = lambda u, v: jnp.dot(u, v, preferred_element_type=jnp.float32)
    return dot(a_hi, b_hi) + dot(a_hi, b_lo) + dot(a_lo, b_hi)


def kernel(dens, pat_in, wts_in, out, chk, dcol, drow, srow, hop, acc, pat, wts,
           sums_out, sums_in, parts_out, parts_in, load, send, recv):
    row, col = lax.axis_index("row"), lax.axis_index("col")
    x, yh = row // 2, row % 2
    z, yl, core = col // 4, (col // 2) % 2, col % 2

    def dev(x_, yh_, z_, yl_, core_):
        return (x_ * 2 + yh_, (z_ * 2 + yl_) * 2 + core_)

    def step(value, by):
        return (value + by) % 4

    def rowslot(x_, yh_):
        return x_ * 2 + yh_

    def colslot(z_, yl_):
        return (z_ * 2 + yl_) * 2 + core

    peer = {
        "x+": dev(step(x, 1), yh, z, yl, core), "x-": dev(step(x, 3), yh, z, yl, core),
        "z+": dev(x, yh, step(z, 1), yl, core), "z-": dev(x, yh, step(z, 3), yl, core),
        "ya": dev(x, yh, z, 1 - yl, core), "yb": dev(x, 1 - yh, z, 1 - yl, core),
        "mate": dev(x, yh, z, yl, 1 - core),
    }
    rows_of = [((row + i) % NROW, col) for i in range(1, NROW)]
    cols_of = [(row, (col + i) % NCOL) for i in range(1, NCOL)]

    barrier = pltpu.get_barrier_semaphore()
    greet = list(peer.values())
    for device in greet:
        pl.semaphore_signal(barrier, inc=1, device_id=device, device_id_type=MESH)
    loads = [pltpu.make_async_copy(src, dst, load.at[i]) for i, (src, dst) in enumerate((
        (pat_in, pat), (wts_in, wts), (dens, drow.at[col]), (dens, dcol.at[row])))]
    for copy in loads:
        copy.start()
    for copy in loads[:2]:
        copy.wait()

    acc[...] = jnp.zeros_like(acc)
    nr, nc = ROWS // BLK, COLS // BLK
    rm = (lax.broadcasted_iota(jnp.int32, (nr, ROWS), 0)
          == lax.broadcasted_iota(jnp.int32, (nr, ROWS), 1) // BLK)
    cm = (lax.broadcasted_iota(jnp.int32, (COLS, nc), 1)
          == lax.broadcasted_iota(jnp.int32, (COLS, nc), 0) // BLK)
    part = jnp.dot(cm.astype(jnp.float32), pat[...].astype(jnp.float32),
                   preferred_element_type=jnp.float32)
    mask = jnp.dot(part, rm.astype(jnp.float32), preferred_element_type=jnp.float32)

    w_col = jnp.broadcast_to(wts[...][None, :], (128, ROWS)).T

    def column_sums(value):
        return dot3(value, w_col).T[:8]

    for copy in loads[2:]:
        copy.wait()
    pl.semaphore_wait(barrier, len(greet))

    copies = {}

    def put(name, src, dst, device):
        i = len(copies)
        copies[name] = pltpu.make_async_remote_copy(
            src_ref=src, dst_ref=dst, send_sem=send.at[i], recv_sem=recv.at[i],
            device_id=device, device_id_type=MESH)
        copies[name].start()

    def wait(name):
        copies[name].wait_recv()

    rowslots = {
        "mine": row, "back": rowslot(step(x, 3), yh), "ahead": rowslot(step(x, 1), yh),
        "far": rowslot(step(x, 2), yh), "mine_p": rowslot(x, 1 - yh),
        "back_p": rowslot(step(x, 3), 1 - yh), "ahead_p": rowslot(step(x, 1), 1 - yh),
        "far_p": rowslot(step(x, 2), 1 - yh),
    }
    colslots = {
        "mine": col, "back": colslot(step(z, 3), yl), "ahead": colslot(step(z, 1), yl),
        "far": colslot(step(z, 2), yl), "mine_p": colslot(z, 1 - yl),
        "back_p": colslot(step(z, 3), 1 - yl), "ahead_p": colslot(step(z, 1), 1 - yl),
        "far_p": colslot(step(z, 2), 1 - yl),
    }

    def panel_copy(buf, slots):
        def make(name, link, src, dst, first, rows, i, p):
            ref = buf.at[slots[src], pl.ds(first, rows), :]
            return lambda _: put(name, ref, ref, peer[link])
        return make

    def column_copy(name, link, src, dst, first, rows, i, p):
        span = pl.ds(first, rows)
        here = dcol.at[rowslots[src], span, :]
        if link in ("x+", "x-"):
            return lambda _: put(name, here, here, peer[link])
        place = ("mine", "back", "ahead", "far").index(src)
        between = hop.at[place, span, :]
        if i == 0:
            return lambda _: put(name, here, between, peer[link])
        origin = rowslot(step(x, (0, 3, 1, 2)[place]), yh if link == "yb" else 1 - yh)
        there = dcol.at[origin, span, :]
        return lambda _: put(name, between, there, peer[link])

    def mates(tag, buf, fills, pieces, start=lambda half: []):
        given = {"mine": []}
        for half, (first, rows) in enumerate(GROUPS):
            name = f"{tag}m{first}"
            ref = buf.at[col, pl.ds(first, rows), :]
            plan.add(name, "mate", rows, start(half), lambda _, n=name, r=ref: put(n, r, r, peer["mate"]))
            given["mine"].append(name)
        for slot, by in fills.items():
            given[slot] = []
            groups = [q[:2] for q in pieces] if slot == "far_p" else GROUPS
            for first, rows in groups:
                deps = [by[p] for p, q in enumerate(pieces) if first <= q[0] < first + rows]
                name = f"{tag}m{slot}{first}"
                ref = buf.at[colslots[slot], pl.ds(first, rows), :]
                plan.add(name, "mate", rows, deps, lambda _, n=name, r=ref: put(n, r, r, peer["mate"]))
                given[slot].append(name)
        return {slot: list(by.values()) + given[slot] for slot, by in fills.items()} | {"mine": given["mine"]}

    def product(panel, k, which, first=0, rows=COLS):
        def do(_):
            span = pl.ds(first, rows)
            acc[which, span, :] += dot3(dcol[k, span, :], panel[pl.ds(2 * k, 2)].reshape(2 * COLS, ROWS))
        return do

    plan = Plan()
    fill_c = ring(plan, "C", PIECES_C, "x+", "x-",
                  lambda p: ("ya", "yb") if PIECES_C[p][3] > 0 else ("yb", "ya"), column_copy)
    fill_r = ring(plan, "R", PIECES_R, "z+", "z-", lambda p: ("ya",), panel_copy(drow, colslots))
    have = mates("R", drow, fill_r, PIECES_R)

    def need(r_slots, c_slots):
        return ([n for s in r_slots for n in have[s]] + [n for s in c_slots for n in fill_c[s].values()])

    d, even = (z - x + 4) % 4, yl == yh
    ny = 1 - yl
    o0 = jnp.where(d == 2, step(x, 1), x)
    o1 = jnp.where(d <= 1, step(x, 1), step(x, 3))
    o2 = jnp.where(d == 0, step(x, 3), step(z, 2))
    o3 = step(x, 2)
    sel = lambda a, b: jnp.where(even, a, b)
    stage1 = [rowslot(x, yl), sel(rowslot(step(x, 1), yl), rowslot(z, yh))]
    stage2 = [sel(rowslot(step(x, 2), yl), rowslot(step(x, 1), yl)), rowslot(step(x, 3), yl),
              sel(rowslot(o0, ny), rowslot(step(z, 1), yh)), sel(rowslot(o1, ny), rowslot(step(z, 3), yh))]
    stage3 = [sel(rowslot(o2, ny), rowslot(step(x, 2), yl)), sel(rowslot(o3, ny), rowslot(step(z, 2), yh))]
    own, par = ["back", "ahead", "far"], ["mine_p", "back_p", "ahead_p"]
    needs = (
        (["mine"] + own, ["mine_p"]), (["mine"] + own + ["mine_p"], own),
        (["mine"] + own, ["far", "ahead_p"]), (["mine"] + own, ["back", "back_p"]),
        (par, own + ["mine_p", "ahead_p"]), (par, own + ["ahead_p", "back_p"]),
        (["mine"] + own + par + ["far_p"], own + par + ["far_p"]), ([], []),
    )
    deps = []
    blocks = stage1 + stage2 + stage3
    for i, (k, slots) in enumerate(zip(blocks[:6], needs)):
        deps = deps + need(*slots)
        plan.add(f"work{i}", "work", 1.3, deps, product(drow, k, 0))
        deps = deps + [f"work{i}"]
    deps = deps + need(*needs[6])

    def square(first, rows):
        def do(_):
            span = pl.ds(first, rows)
            srow[col, span, :] = mask[first:first + rows] * acc[0, span, :]
        return do

    for half, (first, rows) in enumerate(GROUPS):
        for i in (6, 7):
            plan.add(f"work{i}/{half}", "work", 0.75, deps, product(drow, blocks[i], 0, first, rows))
            deps = deps + [f"work{i}/{half}"]
        plan.add(f"square{half}", "work", 0.4, deps, square(first, rows))
        deps = deps + [f"square{half}"]

    def squared(half):
        return [f"square{half}"]

    fill_s = ring(plan, "S", PIECES_S, "z+", "z-", lambda p: ("ya",), panel_copy(srow, colslots),
                  lambda p: squared(PIECES_S[p][0] // GROUPS[0][1]))
    have = mates("S", srow, fill_s, PIECES_S, squared)

    def sums(_):
        first = lax.broadcasted_iota(jnp.int32, (8, COLS), 0) == 0
        value = jnp.where(first, column_sums(acc[0]), column_sums(srow[col]))
        sums_out[0] = value
        sums_in[row] = value
        for i, device in enumerate(rows_of):
            put(f"sums{i}", sums_out.at[0], sums_in.at[row], device)

    def total_sums(_):
        for i in range(NROW - 1):
            wait(f"sums{i}")
        total = sums_in[0]
        for i in range(1, NROW):
            total += sums_in[i]
        chk[0:1, :] = total[0:1]
        sums_out[1] = total

    def parts(first):
        def do(_):
            def run(k, carry):
                value = dot3(sums_out[1], dcol[k])
                parts_out[2 * k] = value[:, :COLS]
                parts_out[2 * k + 1] = value[:, COLS:]
                return carry

            lax.fori_loop(first, first + 2, run, 0)
        return do

    def spread(_):
        parts_in[col] = parts_out[col]
        for i, device in enumerate(cols_of):
            put(f"parts{i}", parts_out.at[device[1]], parts_in.at[col], device)

    plan.add("sums", "work", 2.0, ["square1"], sums)
    plan.add("total", "work", 0.3, list(fill_s["back"].values()) + ["sums"], total_sums)
    for k in range(0, NROW, 2):
        plan.add(f"parts{k}", "work", 1.6, ["total" if k == 0 else f"parts{k - 2}"], parts(k))
    plan.add("spread", "work", 0.3, ["parts6"], spread)
    places = {"mine": (0, yl), "back": (3, yl), "ahead": (1, yl), "far": (2, yl)}
    places |= {f"{slot}_p": (by, 1 - y) for slot, (by, y) in places.items()}
    for slot, (by, y) in places.items():
        plan.add(f"work_{slot}", "work", 1.3, have[slot] + ["square1"],
                 product(srow, rowslot(step(z, by), y), 1))
    plan.run(wait)

    out[...] = 3.0 * srow[col] - 2.0 * (mask * acc[1])
    for i in range(NCOL - 1):
        wait(f"parts{i}")
    total = parts_in[0]
    for i in range(1, NCOL):
        total += parts_in[i]
    chk[1:2, :] = total[1:2]
    for copy in copies.values():
        copy.wait_send()
    assert len(copies) <= SEMS, len(copies)


def body(density, pattern, weights):
    f32 = jnp.float32
    vmem = pl.BlockSpec(memory_space=pltpu.VMEM)
    hbm = pl.BlockSpec(memory_space=pltpu.HBM)
    purified, checks = pl.pallas_call(
        kernel,
        out_shape=(jax.ShapeDtypeStruct((COLS, ROWS), f32), jax.ShapeDtypeStruct((2, COLS), f32)),
        in_specs=[hbm] * 3,
        out_specs=(vmem, vmem),
        scratch_shapes=[
            pltpu.VMEM((NROW, COLS, ROWS), f32),
            pltpu.VMEM((NCOL, COLS, ROWS), f32),
            pltpu.VMEM((NCOL, COLS, ROWS), f32),
            pltpu.VMEM((4, COLS, ROWS), f32),
            pltpu.VMEM((2, COLS, ROWS), f32),
            pltpu.VMEM((COLS // BLK, ROWS // BLK), jnp.int32),
            pltpu.VMEM((ROWS,), f32),
            pltpu.VMEM((2, 8, COLS), f32),
            pltpu.VMEM((NROW, 8, COLS), f32),
            pltpu.VMEM((NCOL, 8, COLS), f32),
            pltpu.VMEM((NCOL, 8, COLS), f32),
            pltpu.SemaphoreType.DMA((4,)),
            pltpu.SemaphoreType.DMA((SEMS,)),
            pltpu.SemaphoreType.DMA((SEMS,)),
        ],
        compiler_params=pltpu.CompilerParams(
            collective_id=0, has_side_effects=True, vmem_limit_bytes=46 * 1024 * 1024),
        name="purify",
    )(*(pltpu.with_memory_space_constraint(a, pltpu.HBM) for a in (density.T, pattern.T, weights)))
    return purified.T, checks


def solution(mesh):
    in_specs = (P("row", "col"), P("row", "col"), P("row"))
    out_specs = (P("row", "col"), P(None, "col"))
    return jax.shard_map(body, mesh=mesh, in_specs=in_specs, out_specs=out_specs, check_vma=False)
```

```python
import jax
import jax.numpy as jnp
from jax import lax
from jax.experimental import pallas as pl
from jax.experimental.pallas import tpu as pltpu
from jax.sharding import PartitionSpec as P

BLK = 64
MESH = pl.DeviceIdType.MESH
ROWS, COLS = 640, 320
NROW, NCOL = 8, 16
SEMS = 240

LINK_ROW, LINK_LATENCY = 0.0545, 3.0
MATE_ROW, MATE_LATENCY = 0.0057, 1.0
LEAD, PATIENCE, ISSUE = 3.0, 0.5, 0.02

PIECES_C = ((0, 16, "after", 1), (16, 48, "first", 1), (64, 96, "first", 1),
            (160, 16, "after", -1), (176, 48, "first", -1), (224, 96, "first", -1))
PIECES_R = ((0, 32, "first", 1), (32, 32, "first", 1), (64, 72, "first", 1), (136, 24, "after", 1),
            (160, 32, "first", -1), (192, 32, "first", -1), (224, 72, "first", -1), (296, 24, "after", -1))
PIECES_S = ((0, 88, "first", 1), (88, 72, "after", 1), (160, 88, "first", -1), (248, 72, "after", -1))
GROUPS = ((0, 160), (160, 160))


class Plan:
    def __init__(self):
        self.items, self.made = {}, {}

    def add(self, name, link, rows, deps, do):
        if link == "work":
            length, latency = rows, 0.0
        elif link == "mate":
            length, latency = rows * MATE_ROW, MATE_LATENCY
        else:
            length, latency = rows * LINK_ROW, LINK_LATENCY
        self.items[name] = (link, length, latency, tuple(deps), do)

    def order(self):
        items = self.items
        after = {name: [] for name in items}
        for name, item in items.items():
            for dep in item[3]:
                after[dep].append(name)
        level = {}
        for name in reversed(list(items)):
            _, length, latency, _, _ = items[name]
            level[name] = length + latency + max([level[n] for n in after[name]], default=0.0)
        now, free, there, program = 0.0, {}, {}, []
        left = sorted(items, key=lambda name: -level[name])
        while left:
            ready = {}
            for name in left:
                deps = items[name][3]
                if all(dep in there for dep in deps):
                    ready[name] = max([there[dep] for dep in deps], default=0.0)
            chosen, following = None, []
            for name, since in ready.items():
                link = items[name][0]
                if link == "work":
                    if since > now:
                        following.append(since)
                    continue
                since = max(since, free.get(link, 0.0) - LEAD)
                if since <= now:
                    chosen = name
                    break
                following.append(since)
            if chosen is None:
                for name, since in ready.items():
                    link, length = items[name][:2]
                    if link != "work" or since > now:
                        continue
                    idle = max([now + length - max(free.get(items[n][0], 0.0), t)
                                for n, t in ready.items() if items[n][0] not in ("work", "mate")],
                               default=0.0)
                    if idle <= PATIENCE:
                        chosen = name
                        break
            if chosen is None:
                if following:
                    now = min(following)
                    continue
                chosen = next(iter(ready))
            link, length, latency, _, _ = items[chosen]
            if link == "work":
                now += length
                there[chosen] = now
            else:
                free[link] = max(now, free.get(link, 0.0)) + length
                there[chosen] = free[link] + latency
                now += ISSUE
            program.append(chosen)
            left.remove(chosen)
        return program, there

    def run(self, wait):
        done = set()
        for name in self.order()[0]:
            _, _, _, deps, do = self.items[name]
            for dep in deps:
                if dep not in done and self.items[dep][0] != "work":
                    wait(dep)
                    done.add(dep)
            do(name)
        for name in self.items:
            if name not in done and self.items[name][0] != "work":
                wait(name)


def ring(plan, tag, pieces, plus, minus, cross, send_to, start=lambda p: []):
    fills = {slot: {} for slot in ("back", "ahead", "far", "mine_p", "back_p", "ahead_p", "far_p")}

    def over(name, src, dst, p, deps):
        first, rows = pieces[p][:2]
        last = deps
        for i, link in enumerate(cross(p)):
            step = f"{name}/{i}"
            plan.add(step, link, rows, last, send_to(step, link, src, dst, first, rows, i, p))
            last = [step]
        fills[dst][p] = last[0]
        return last

    def around(kind, p, deps, slots):
        mine, back, ahead, far = slots
        first, rows, _, way = pieces[p]
        names = {}
        for link, dst in ((plus, back), (minus, ahead)):
            name = f"{tag}{kind}{link}{p}"
            plan.add(name, link, rows, deps, send_to(name, link, mine, dst, first, rows, 0, p))
            fills[dst][p] = name
            names[link] = name
        link, src = (plus, back) if way > 0 else (minus, ahead)
        name = f"{tag}{kind}far{p}"
        plan.add(name, link, rows, [names[link]], send_to(name, link, src, far, first, rows, 0, p))
        fills[far][p] = name

    for p, (first, rows, when, way) in enumerate(pieces):
        around("own", p, start(p), ("mine", "back", "ahead", "far"))
        if when == "first":
            last = over(f"{tag}y{p}", "mine", "mine_p", p, start(p))
            around("par", p, last, ("mine_p", "back_p", "ahead_p", "far_p"))
        else:
            over(f"{tag}y{p}", "mine", "mine_p", p, start(p))
            for slot in ("back", "ahead", "far"):
                over(f"{tag}y{slot}{p}", slot, slot + "_p", p, [fills[slot][p]])
    return fills


def split(value):
    high = value.astype(jnp.bfloat16)
    low = (value - high.astype(jnp.float32)).astype(jnp.bfloat16)
    return high, low


def dot3(a, b):
    (a_hi, a_lo), (b_hi, b_lo) = split(a), split(b)
    dot = lambda u, v: jnp.dot(u, v, preferred_element_type=jnp.float32)
    return dot(a_hi, b_hi) + dot(a_hi, b_lo) + dot(a_lo, b_hi)


def kernel(dens, pat_in, wts_in, out, chk, dcol, drow, srow, hop, acc, pat, wts,
           sums_out, sums_in, parts_out, parts_in, load, send, recv):
    row, col = lax.axis_index("row"), lax.axis_index("col")
    x, yh = row // 2, row % 2
    z, yl, core = col // 4, (col // 2) % 2, col % 2

    def dev(x_, yh_, z_, yl_, core_):
        return (x_ * 2 + yh_, (z_ * 2 + yl_) * 2 + core_)

    def step(value, by):
        return (value + by) % 4

    def rowslot(x_, yh_):
        return x_ * 2 + yh_

    def colslot(z_, yl_):
        return (z_ * 2 + yl_) * 2 + core

    peer = {
        "x+": dev(step(x, 1), yh, z, yl, core), "x-": dev(step(x, 3), yh, z, yl, core),
        "z+": dev(x, yh, step(z, 1), yl, core), "z-": dev(x, yh, step(z, 3), yl, core),
        "ya": dev(x, yh, z, 1 - yl, core), "yb": dev(x, 1 - yh, z, 1 - yl, core),
        "mate": dev(x, yh, z, yl, 1 - core),
    }
    rows_of = [((row + i) % NROW, col) for i in range(1, NROW)]
    cols_of = [(row, (col + i) % NCOL) for i in range(1, NCOL)]

    barrier = pltpu.get_barrier_semaphore()
    greet = list(peer.values())
    for device in greet:
        pl.semaphore_signal(barrier, inc=1, device_id=device, device_id_type=MESH)
    loads = [pltpu.make_async_copy(src, dst, load.at[i]) for i, (src, dst) in enumerate((
        (pat_in, pat), (wts_in, wts), (dens, drow.at[col]), (dens, dcol.at[row])))]
    for copy in loads:
        copy.start()
    for copy in loads[:2]:
        copy.wait()

    acc[...] = jnp.zeros_like(acc)
    nr, nc = ROWS // BLK, COLS // BLK
    rm = (lax.broadcasted_iota(jnp.int32, (nr, ROWS), 0)
          == lax.broadcasted_iota(jnp.int32, (nr, ROWS), 1) // BLK)
    cm = (lax.broadcasted_iota(jnp.int32, (COLS, nc), 1)
          == lax.broadcasted_iota(jnp.int32, (COLS, nc), 0) // BLK)
    part = jnp.dot(cm.astype(jnp.float32), pat[...].astype(jnp.float32),
                   preferred_element_type=jnp.float32)
    mask = jnp.dot(part, rm.astype(jnp.float32), preferred_element_type=jnp.float32)

    w_col = jnp.broadcast_to(wts[...][None, :], (128, ROWS)).T

    def column_sums(value):
        return dot3(value, w_col).T[:8]

    for copy in loads[2:]:
        copy.wait()
    pl.semaphore_wait(barrier, len(greet))

    copies = {}

    def put(name, src, dst, device):
        i = len(copies)
        copies[name] = pltpu.make_async_remote_copy(
            src_ref=src, dst_ref=dst, send_sem=send.at[i], recv_sem=recv.at[i],
            device_id=device, device_id_type=MESH)
        copies[name].start()

    def wait(name):
        copies[name].wait_recv()

    rowslots = {
        "mine": row, "back": rowslot(step(x, 3), yh), "ahead": rowslot(step(x, 1), yh),
        "far": rowslot(step(x, 2), yh), "mine_p": rowslot(x, 1 - yh),
        "back_p": rowslot(step(x, 3), 1 - yh), "ahead_p": rowslot(step(x, 1), 1 - yh),
        "far_p": rowslot(step(x, 2), 1 - yh),
    }
    colslots = {
        "mine": col, "back": colslot(step(z, 3), yl), "ahead": colslot(step(z, 1), yl),
        "far": colslot(step(z, 2), yl), "mine_p": colslot(z, 1 - yl),
        "back_p": colslot(step(z, 3), 1 - yl), "ahead_p": colslot(step(z, 1), 1 - yl),
        "far_p": colslot(step(z, 2), 1 - yl),
    }

    def panel_copy(buf, slots):
        def make(name, link, src, dst, first, rows, i, p):
            ref = buf.at[slots[src], pl.ds(first, rows), :]
            return lambda _: put(name, ref, ref, peer[link])
        return make

    def column_copy(name, link, src, dst, first, rows, i, p):
        span = pl.ds(first, rows)
        here = dcol.at[rowslots[src], span, :]
        if link in ("x+", "x-"):
            return lambda _: put(name, here, here, peer[link])
        place = ("mine", "back", "ahead", "far").index(src)
        between = hop.at[place, span, :]
        if i == 0:
            return lambda _: put(name, here, between, peer[link])
        origin = rowslot(step(x, (0, 3, 1, 2)[place]), yh if link == "yb" else 1 - yh)
        there = dcol.at[origin, span, :]
        return lambda _: put(name, between, there, peer[link])

    def mates(tag, buf, fills, pieces, start=lambda half: []):
        given = {"mine": []}
        for half, (first, rows) in enumerate(GROUPS):
            name = f"{tag}m{first}"
            ref = buf.at[col, pl.ds(first, rows), :]
            plan.add(name, "mate", rows, start(half), lambda _, n=name, r=ref: put(n, r, r, peer["mate"]))
            given["mine"].append(name)
        for slot, by in fills.items():
            given[slot] = []
            groups = [q[:2] for q in pieces] if slot == "far_p" else GROUPS
            for first, rows in groups:
                deps = [by[p] for p, q in enumerate(pieces) if first <= q[0] < first + rows]
                name = f"{tag}m{slot}{first}"
                ref = buf.at[colslots[slot], pl.ds(first, rows), :]
                plan.add(name, "mate", rows, deps, lambda _, n=name, r=ref: put(n, r, r, peer["mate"]))
                given[slot].append(name)
        return {slot: list(by.values()) + given[slot] for slot, by in fills.items()} | {"mine": given["mine"]}

    def product(panel, k, which, first=0, rows=COLS):
        def do(_):
            span = pl.ds(first, rows)
            acc[which, span, :] += dot3(dcol[k, span, :], panel[pl.ds(2 * k, 2)].reshape(2 * COLS, ROWS))
        return do

    plan = Plan()
    fill_c = ring(plan, "C", PIECES_C, "x+", "x-",
                  lambda p: ("ya", "yb") if PIECES_C[p][3] > 0 else ("yb", "ya"), column_copy)
    fill_r = ring(plan, "R", PIECES_R, "z+", "z-", lambda p: ("ya",), panel_copy(drow, colslots))
    have = mates("R", drow, fill_r, PIECES_R)

    def need(r_slots, c_slots):
        return ([n for s in r_slots for n in have[s]] + [n for s in c_slots for n in fill_c[s].values()])

    d, even = (z - x + 4) % 4, yl == yh
    ny = 1 - yl
    o0 = jnp.where(d == 2, step(x, 1), x)
    o1 = jnp.where(d <= 1, step(x, 1), step(x, 3))
    o2 = jnp.where(d == 0, step(x, 3), step(z, 2))
    o3 = step(x, 2)
    sel = lambda a, b: jnp.where(even, a, b)
    stage1 = [rowslot(x, yl), sel(rowslot(step(x, 1), yl), rowslot(z, yh))]
    stage2 = [sel(rowslot(step(x, 2), yl), rowslot(step(x, 1), yl)), rowslot(step(x, 3), yl),
              sel(rowslot(o0, ny), rowslot(step(z, 1), yh)), sel(rowslot(o1, ny), rowslot(step(z, 3), yh))]
    stage3 = [sel(rowslot(o2, ny), rowslot(step(x, 2), yl)), sel(rowslot(o3, ny), rowslot(step(z, 2), yh))]
    own, par = ["back", "ahead", "far"], ["mine_p", "back_p", "ahead_p"]
    needs = (
        (["mine"] + own, ["mine_p"]), (["mine"] + own + ["mine_p"], own),
        (["mine"] + own, ["far", "ahead_p"]), (["mine"] + own, ["back", "back_p"]),
        (par, own + ["mine_p", "ahead_p"]), (par, own + ["ahead_p", "back_p"]),
        (["mine"] + own + par + ["far_p"], own + par + ["far_p"]), ([], []),
    )
    deps = []
    blocks = stage1 + stage2 + stage3
    for i, (k, slots) in enumerate(zip(blocks[:6], needs)):
        deps = deps + need(*slots)
        plan.add(f"work{i}", "work", 1.3, deps, product(drow, k, 0))
        deps = deps + [f"work{i}"]
    deps = deps + need(*needs[6])

    def square(first, rows):
        def do(_):
            span = pl.ds(first, rows)
            srow[col, span, :] = mask[first:first + rows] * acc[0, span, :]
        return do

    for half, (first, rows) in enumerate(GROUPS):
        for i in (6, 7):
            plan.add(f"work{i}/{half}", "work", 0.75, deps, product(drow, blocks[i], 0, first, rows))
            deps = deps + [f"work{i}/{half}"]
        plan.add(f"square{half}", "work", 0.4, deps, square(first, rows))
        deps = deps + [f"square{half}"]

    def squared(half):
        return [f"square{half}"]

    fill_s = ring(plan, "S", PIECES_S, "z+", "z-", lambda p: ("ya",), panel_copy(srow, colslots),
                  lambda p: squared(PIECES_S[p][0] // GROUPS[0][1]))
    have = mates("S", srow, fill_s, PIECES_S, squared)

    def sums(_):
        first = lax.broadcasted_iota(jnp.int32, (8, COLS), 0) == 0
        value = jnp.where(first, column_sums(acc[0]), column_sums(srow[col]))
        sums_out[0] = value
        sums_in[row] = value
        for i, device in enumerate(rows_of):
            put(f"sums{i}", sums_out.at[0], sums_in.at[row], device)

    def total_sums(_):
        for i in range(NROW - 1):
            wait(f"sums{i}")
        total = sums_in[0]
        for i in range(1, NROW):
            total += sums_in[i]
        chk[0:1, :] = total[0:1]
        sums_out[1] = total

    def parts(first):
        def do(_):
            def run(k, carry):
                value = dot3(sums_out[1], dcol[k])
                parts_out[2 * k] = value[:, :COLS]
                parts_out[2 * k + 1] = value[:, COLS:]
                return carry

            lax.fori_loop(first, first + 2, run, 0)
        return do

    def spread(_):
        parts_in[col] = parts_out[col]
        for i, device in enumerate(cols_of):
            put(f"parts{i}", parts_out.at[device[1]], parts_in.at[col], device)

    plan.add("sums", "work", 2.0, ["square1"], sums)
    plan.add("total", "work", 0.3, list(fill_s["back"].values()) + ["sums"], total_sums)
    for k in range(0, NROW, 2):
        plan.add(f"parts{k}", "work", 1.6, ["total" if k == 0 else f"parts{k - 2}"], parts(k))
    plan.add("spread", "work", 0.3, ["parts6"], spread)
    places = {"mine": (0, yl), "back": (3, yl), "ahead": (1, yl), "far": (2, yl)}
    places |= {f"{slot}_p": (by, 1 - y) for slot, (by, y) in places.items()}
    for slot, (by, y) in places.items():
        plan.add(f"work_{slot}", "work", 1.3, have[slot] + ["square1"],
                 product(srow, rowslot(step(z, by), y), 1))
    plan.run(wait)

    out[...] = 3.0 * srow[col] - 2.0 * (mask * acc[1])
    for i in range(NCOL - 1):
        wait(f"parts{i}")
    total = parts_in[0]
    for i in range(1, NCOL):
        total += parts_in[i]
    chk[1:2, :] = total[1:2]
    for copy in copies.values():
        copy.wait_send()
    assert len(copies) <= SEMS, len(copies)


def body(density, pattern, weights):
    f32 = jnp.float32
    vmem = pl.BlockSpec(memory_space=pltpu.VMEM)
    hbm = pl.BlockSpec(memory_space=pltpu.HBM)
    purified, checks = pl.pallas_call(
        kernel,
        out_shape=(jax.ShapeDtypeStruct((COLS, ROWS), f32), jax.ShapeDtypeStruct((2, COLS), f32)),
        in_specs=[hbm] * 3,
        out_specs=(vmem, vmem),
        scratch_shapes=[
            pltpu.VMEM((NROW, COLS, ROWS), f32),
            pltpu.VMEM((NCOL, COLS, ROWS), f32),
            pltpu.VMEM((NCOL, COLS, ROWS), f32),
            pltpu.VMEM((4, COLS, ROWS), f32),
            pltpu.VMEM((2, COLS, ROWS), f32),
            pltpu.VMEM((COLS // BLK, ROWS // BLK), jnp.int32),
            pltpu.VMEM((ROWS,), f32),
            pltpu.VMEM((2, 8, COLS), f32),
            pltpu.VMEM((NROW, 8, COLS), f32),
            pltpu.VMEM((NCOL, 8, COLS), f32),
            pltpu.VMEM((NCOL, 8, COLS), f32),
            pltpu.SemaphoreType.DMA((4,)),
            pltpu.SemaphoreType.DMA((SEMS,)),
            pltpu.SemaphoreType.DMA((SEMS,)),
        ],
        compiler_params=pltpu.CompilerParams(
            collective_id=0, has_side_effects=True, vmem_limit_bytes=46 * 1024 * 1024),
        name="purify",
    )(*(pltpu.with_memory_space_constraint(a, pltpu.HBM) for a in (density.T, pattern.T, weights)))
    return purified.T, checks


def solution(mesh):
    in_specs = (P("row", "col"), P("row", "col"), P("row"))
    out_specs = (P("row", "col"), P(None, "col"))
    return jax.shard_map(body, mesh=mesh, in_specs=in_specs, out_specs=out_specs, check_vma=False)
```
